128 devices in a mesh: tm: 64 (over z_hi, x, y, core), inp: 2 (over z_lo).
Axes of the slice: x: 4, y: 4, z: 4 (z_hi: 2, z_lo: 2; z = z_hi * 2 + z_lo), core: 2. Of those that a mesh axis runs over, the one named last changes fastest.
Arguments:
- voltages: bfloat16 [2, 262144, 1024], P(None, 'tm', 'inp'), may hold values from -127 to 127, as said below
- taps: int32 [12, 1024], replicated, may hold values from -64 to 64
Outputs:
- visibility: bfloat16 [512, 1024, 1024], P(('tm', 'inp'))
The draws below stay inside these ranges and needn't reach their ends.
Inputs may be any that keep to these rules, and one draw needn't show every extreme that they name: `voltages`: every sample is a whole number.
All inputs are finite; a program needn't handle non-finite values.
Results may differ from the reference program's by a relative error of at most 0.0048.
Values may be sent and summed in bfloat16 or wider, within the bound.
A program may use at most 576 MiB of HBM per device.

```python
import math
import jax
import jax.numpy as jnp
from jax import lax

INPUTS = 1024
FINE = 1024
KEEP = 512
TAPS = 12
NSPEC = 256
SAMPLES = 262144


def draw_voltages(key, part):
    base_key = jax.random.fold_in(key, 7)
    key_list = jax.random.split(base_key, 4)
    amplitude = jax.random.randint(key_list[0], (1, 1, INPUTS), 16, 96)
    noise_part = jax.random.randint(key_list[1], (2, SAMPLES, INPUTS), -amplitude, amplitude + 1)
    sky_signal = jax.random.randint(key_list[2], (2, SAMPLES, 1), -16, 17)
    sky_weight = jax.random.randint(key_list[3], (1, 1, INPUTS), -2, 3)
    return (noise_part + sky_weight * sky_signal).astype(jnp.float32).astype(jnp.bfloat16)


def touch_ends(drawn, key, smallest, top_value):
    shape = drawn.shape
    spot = [jax.random.randint(jax.random.fold_in(key, axis), (), 0, shape[axis]) for axis in range(len(shape))]
    drawn = drawn.at[tuple(spot)].set(smallest)
    longest = shape.index(max(shape))
    spot[longest] = (spot[longest] + 1) % shape[longest]
    return drawn.at[tuple(spot)].set(top_value)


def setup_inputs(seed: int = 0) -> dict:
    splits = jax.random.split(jax.random.key(seed), 3)
    voltages = draw_voltages(jax.random.fold_in(splits[2], 71), 0)
    taps = touch_ends(jax.random.randint(splits[1], (TAPS, FINE), -64, 65), jax.random.fold_in(splits[1], 1), -64, 64).astype(jnp.int32)
    return dict(voltages=voltages, taps=taps)


def dft_table(fine_count, keep_count):
    branch = jnp.arange(fine_count, dtype=jnp.int32)[:, None]
    channel = jnp.arange(keep_count, dtype=jnp.int32)[None, :] - keep_count // 2
    phase_index = jnp.mod(branch * channel, fine_count).astype(jnp.float32)
    angles = 2.0 * math.pi / fine_count * phase_index
    norm_scale = 1.0 / math.sqrt(fine_count)
    cosine = jnp.cos(angles) * norm_scale
    sine_part = jnp.sin(angles) * norm_scale
    dft_matrix = jnp.stack([jnp.stack([cosine, -sine_part], 1), jnp.stack([sine_part, cosine], 1)], 0)
    return dft_matrix.astype(jnp.bfloat16)

def reference(voltages, taps):
    history_len = TAPS - 1
    dft_matrix = dft_table(FINE, KEEP).astype(jnp.float32)
    coefficient = taps.astype(jnp.float32)
    block_count = max(INPUTS // 128, 1)
    block_width = INPUTS // block_count
    volt_blocks = voltages.reshape(2, NSPEC, FINE, block_count, block_width).transpose(3, 0, 1, 2, 4)

    def spectra_of(volt_block):
        padded = jnp.pad(volt_block.astype(jnp.float32), ((0, 0), (history_len, 0), (0, 0), (0, 0)))
        filtered = jnp.zeros((2, NSPEC, FINE, block_width), jnp.float32)
        for k in range(TAPS):
            filtered = filtered + coefficient[k][None, None, :, None] * padded[:, history_len - k:history_len - k + NSPEC]
        filtered = (filtered * (1.0 / 8192.0)).astype(jnp.bfloat16)
        spectra_block = jnp.einsum('rfna,rnsj->jsfa', filtered.astype(jnp.float32), dft_matrix)
        return spectra_block.astype(jnp.bfloat16)
    channel_spectra = lax.map(spectra_of, volt_blocks)
    channel_spectra = channel_spectra.transpose(1, 2, 3, 0, 4).reshape(KEEP, 2, NSPEC, INPUTS)
    upper_mask = jnp.arange(INPUTS)[:, None] <= jnp.arange(INPUTS)[None, :]

    def correlate(spectra_one):
        stacked_rows = spectra_one.reshape(2 * NSPEC, INPUTS)
        turned = jnp.concatenate([-spectra_one[1], spectra_one[0]], 0)
        real_part = jnp.dot(stacked_rows.T, stacked_rows, preferred_element_type=jnp.float32)
        imag_part = jnp.dot(stacked_rows.T, turned, preferred_element_type=jnp.float32)
        norm_scale = 1.0 / NSPEC
        return jnp.where(upper_mask, real_part * norm_scale, imag_part * norm_scale).astype(jnp.bfloat16)
    return lax.map(correlate, channel_spectra)
```

```python
import functools
import math

import jax
import jax.numpy as jnp
import numpy as np
from jax import lax
from jax.experimental import pallas as pl
from jax.experimental.pallas import tpu as pltpu
from jax.sharding import PartitionSpec as P

KEEP = 512
MESH = pl.DeviceIdType.MESH


def table_parts(fine, keep):
    chan = np.repeat(np.arange(keep) - keep // 2, 2)
    part = np.tile(np.arange(2), keep)
    low = (chan[:, None] * np.arange(128)[None, :] + part[:, None] * (fine // 4)) % fine
    high = (chan[:, None] * np.arange(0, fine, 128)[None, :]) % fine
    scale = 1.0 / math.sqrt(fine)
    step = 2.0 * np.pi / fine
    return tuple(
        x.astype(np.float32)
        for x in (np.cos(step * low) * scale, np.sin(step * low) * scale, np.cos(step * high), np.sin(step * high))
    )


def dft_rows(fine, keep):
    low_cos, low_sin, high_cos, high_sin = (jnp.asarray(x) for x in table_parts(fine, keep))
    first = high_cos[:, :, None] * low_cos[:, None, :] - high_sin[:, :, None] * low_sin[:, None, :]
    second = high_sin[:, :, None] * low_cos[:, None, :] + high_cos[:, :, None] * low_sin[:, None, :]
    rows = first.shape[0]
    both = jnp.stack([first, second], axis=1)
    return both.reshape(rows, 2 * fine).astype(jnp.bfloat16)


def partial_spectra(frames, fine, history, volt, taps, table, out, samples, filtered, stage, wide_taps, in_sem, send_sem, recv_sem, out_sem):
    me = lax.axis_index("tm")
    core = lax.rem(me, 2)
    other = 1 - core
    partner = me + 1 - 2 * core
    span = 2 * frames
    produced = span + history
    half = samples.shape[3]
    barrier = pltpu.get_barrier_semaphore()
    pl.semaphore_signal(barrier, inc=1, device_id={"tm": partner}, device_id_type=MESH)
    pl.semaphore_wait(barrier, 1)

    def lanes(which):
        return pl.ds(pl.multiple_of(which * half, half), half)

    remote = []
    local = []
    for r in range(2):
        for f in range(frames):
            source = volt.at[r, pl.ds(f * fine, fine)]
            remote.append(
                pltpu.make_async_remote_copy(
                    src_ref=source.at[:, lanes(other)],
                    dst_ref=samples.at[core * frames + f, r],
                    send_sem=send_sem.at[r, f],
                    recv_sem=recv_sem.at[r, f],
                    device_id={"tm": partner},
                    device_id_type=MESH,
                )
            )
            local.append(
                pltpu.make_async_copy(source.at[:, lanes(core)], samples.at[core * frames + f, r], in_sem.at[r, f])
            )
    for copy in remote + local:
        copy.start()
    for copy in local + remote:
        copy.wait()

    rows = 16

    @pl.loop(0, fine // rows)
    def _(step):
        at = pl.ds(pl.multiple_of(step * rows, rows), rows)
        tap_rows = taps[at, :]
        for k in range(history + 1):
            wide_taps[k] = jnp.broadcast_to(tap_rows[:, k : k + 1], (rows, 128))
        for r in range(2):
            for lane in range(half // 128):
                cols = pl.ds(lane * 128, 128)
                held = [samples[i, r, at, cols].astype(jnp.float32) for i in range(span)]
                for f in range(produced):
                    total = None
                    for i in range(span):
                        if 0 <= f - i <= history:
                            term = wide_taps[f - i] * held[i]
                            total = term if total is None else total + term
                    filtered[f, pl.ds(pl.multiple_of(r * fine + step * rows, rows), rows), cols] = total.astype(jnp.bfloat16)

    def write(f, slot):
        return pltpu.make_async_copy(stage.at[slot], out.at[:, f], out_sem.at[slot])

    @pl.loop(0, produced)
    def _(f):
        slot = lax.rem(f, 2)

        @pl.when(f >= 2)
        def _():
            write(f - 2, slot).wait()

        product = jnp.dot(table[...], filtered[f], preferred_element_type=jnp.float32)
        stage[slot] = product.astype(jnp.bfloat16).reshape(stage.shape[1:])
        write(f, slot).start()

    for f in (produced - 2, produced - 1):
        write(f, f % 2).wait()


def correlate(chips, span, history, inverse, received, out, turned_in, spectra, wide):
    width = received.shape[-1]
    groups = received.shape[1]
    total_inputs = groups * width
    frames = chips * span

    @pl.when(pl.program_id(0) == 0)
    def _():
        @pl.loop(0, chips // 2)
        def _(pair):
            for group in range(groups):
                column = (group % 2) * 2 + group // 2
                for lane in range(width // 128):
                    cols = pl.ds(lane * 128, 128)
                    for sub in range(2):
                        chip = pair * 2 + sub
                        for i in range(span):
                            value = received[chip, group, i, :, cols].astype(jnp.float32)
                            back = 1
                            while i + back * span < span + history:
                                earlier = received[jnp.maximum(chip - back, 0), group, i + back * span, :, cols].astype(jnp.float32)
                                value = value + jnp.where(chip >= back, earlier, 0.0)
                                back += 1
                            wide[pl.ds((sub * span + i) * 8, 8), :] = value
                    for row in range(8):
                        picked = wide[pl.ds(row, 2 * span, stride=8), :].astype(jnp.bfloat16)
                        here = pl.ds(pl.multiple_of((row % 2) * frames + pair * (2 * span), 2 * span), 2 * span)
                        there = pl.ds(pl.multiple_of((1 - row % 2) * frames + pair * (2 * span), 2 * span), 2 * span)
                        at = pl.ds(column * width + lane * 128, 128)
                        spectra[row // 2, here, at] = picked
                        turned_in[row // 2, there, at] = -picked if row % 2 else picked

    chan = pl.program_id(0)
    upper = lax.broadcasted_iota(jnp.int32, (width, width), 0) <= lax.broadcasted_iota(jnp.int32, (width, width), 1)
    contract = (((0,), (0,)), ((), ()))
    for a in range(total_inputs // width):
        rows = pl.ds(a * width, width)
        left = spectra[chan, :, rows]
        real = lax.dot_general(left, spectra[chan, :, pl.ds(a * width, total_inputs - a * width)], contract, preferred_element_type=jnp.float32)
        imag = lax.dot_general(left, turned_in[chan, :, pl.ds(0, (a + 1) * width)], contract, preferred_element_type=jnp.float32)
        if a:
            out[0, rows, pl.ds(0, a * width)] = (imag[:, : a * width] * inverse).astype(jnp.bfloat16)
        middle = jnp.where(upper, real[:, :width], imag[:, a * width :])
        out[0, rows, pl.ds(a * width, width)] = (middle * inverse).astype(jnp.bfloat16)
        if (a + 1) * width < total_inputs:
            out[0, rows, pl.ds((a + 1) * width, total_inputs - (a + 1) * width)] = (real[:, width:] * inverse).astype(jnp.bfloat16)


def per_device(voltages, taps):
    history = taps.shape[0] - 1
    fine = taps.shape[1]
    frames = voltages.shape[1] // fine
    width = voltages.shape[2]
    n_time = lax.axis_size("tm")
    n_group = lax.axis_size("inp")
    devices = n_time * n_group
    chans = KEEP // devices
    half = width // 2
    span = 2 * frames
    produced = span + history
    chips = n_time // 2
    scaled = (taps.astype(jnp.float32) * (1.0 / 8192.0)).T
    table = dft_rows(fine, KEEP)
    vmem = pl.BlockSpec(memory_space=pltpu.VMEM)
    hbm = pl.BlockSpec(memory_space=pl.ANY)
    parts = pl.pallas_call(
        functools.partial(partial_spectra, frames, fine, history),
        out_shape=jax.ShapeDtypeStruct((devices, produced, 2 * chans, half), jnp.bfloat16),
        in_specs=[hbm, vmem, vmem],
        out_specs=hbm,
        scratch_shapes=[
            pltpu.VMEM((span, 2, fine, half), jnp.bfloat16),
            pltpu.VMEM((produced, 2 * fine, half), jnp.bfloat16),
            pltpu.VMEM((2, devices, 2 * chans, half), jnp.bfloat16),
            pltpu.VMEM((history + 1, 16, 128), jnp.float32),
            pltpu.SemaphoreType.DMA((2, frames)),
            pltpu.SemaphoreType.DMA((2, frames)),
            pltpu.SemaphoreType.DMA((2, frames)),
            pltpu.SemaphoreType.DMA((2,)),
        ],
        compiler_params=pltpu.CompilerParams(collective_id=0, has_side_effects=True, vmem_limit_bytes=56 * 2**20),
        name="partial_spectra",
    )(voltages, scaled, table)
    flat = parts.reshape(devices, produced * 2 * chans, half)
    moved = lax.all_to_all(flat, ("tm", "inp"), split_axis=0, concat_axis=0, tiled=True)
    received = moved.reshape(chips, 2 * n_group, produced, 2 * chans, half)
    total = width * n_group
    return pl.pallas_call(
        functools.partial(correlate, chips, span, history, 1.0 / (chips * span)),
        out_shape=jax.ShapeDtypeStruct((chans, total, total), jnp.bfloat16),
        grid=(chans,),
        in_specs=[pl.BlockSpec(memory_space=pltpu.VMEM)],
        out_specs=pl.BlockSpec((1, total, total), lambda c: (c, 0, 0)),
        scratch_shapes=[
            pltpu.VMEM((chans, 2 * chips * span, total), jnp.bfloat16),
            pltpu.VMEM((chans, 2 * chips * span, total), jnp.bfloat16),
            pltpu.VMEM((2 * span * 8, 128), jnp.float32),
        ],
        compiler_params=pltpu.CompilerParams(vmem_limit_bytes=56 * 2**20),
        name="correlate",
    )(received)


def solution(mesh):
    placed = (P(None, "tm", "inp"), P())
    return jax.shard_map(
        per_device,
        mesh=mesh,
        in_specs=placed,
        out_specs=P(("tm", "inp"), None, None),
        check_vma=False,
    )
```

```python
import functools
import math

import jax
import jax.numpy as jnp
import numpy as np
from jax import lax
from jax.experimental import pallas as pl
from jax.experimental.pallas import tpu as pltpu
from jax.sharding import PartitionSpec as P

KEEP = 512
MESH = pl.DeviceIdType.MESH


def table_parts(fine, keep):
    chan = np.repeat(np.arange(keep) - keep // 2, 2)
    part = np.tile(np.arange(2), keep)
    low = (chan[:, None] * np.arange(128)[None, :] + part[:, None] * (fine // 4)) % fine
    high = (chan[:, None] * np.arange(0, fine, 128)[None, :]) % fine
    scale = 1.0 / math.sqrt(fine)
    step = 2.0 * np.pi / fine
    return tuple(
        x.astype(np.float32)
        for x in (np.cos(step * low) * scale, np.sin(step * low) * scale, np.cos(step * high), np.sin(step * high))
    )


CHUNKS = (2, 3, 3, 3, 3, 3, 2)
STEP_BACK = 3


class Place:
    def __init__(self):
        time, self.z_lo = lax.axis_index("tm"), lax.axis_index("inp")
        self.core, self.y = lax.rem(time, 2), lax.rem(time // 2, 4)
        self.x, self.z_hi = lax.rem(time // 8, 4), time // 32

    def index(self, z_lo, core, y, x, z_hi):
        return ((z_hi * 4 + x) * 4 + y) * 2 + core, z_lo

    def mixed(self, own, digit):
        low = lax.rem(own + digit, 2)
        high = lax.rem(own // 2 + digit // 2, 2)
        return high * 2 + low

    def flipped(self, flip):
        z_lo, core, y, x, z_hi = flip
        return self.index(
            lax.rem(self.z_lo + z_lo, 2), lax.rem(self.core + core, 2), self.mixed(self.y, y), self.mixed(self.x, x), lax.rem(self.z_hi + z_hi, 2)
        )

    def shifted(self, flip, shift, mix):
        z_lo, core, y, x, z_hi = flip
        moved_y = lax.rem(self.y + shift, 4)
        moved_x = lax.rem(self.x + shift, 4)
        moved_z = lax.rem(self.z_hi * 2 + self.z_lo + shift, 4)
        new_y = moved_y if y == 2 else (self.mixed(self.y, y) if mix else self.y)
        other_x = self.mixed(self.x, x) if mix else self.x
        new_x = jnp.where(x == 2, moved_x, other_x)
        other_lo = lax.rem(self.z_lo + z_lo, 2) if mix else self.z_lo
        other_hi = lax.rem(self.z_hi + z_hi, 2) if mix else self.z_hi
        if z_lo:
            new_lo, new_hi = other_lo, other_hi
        else:
            new_lo = jnp.where(z_hi == 1, lax.rem(moved_z, 2), other_lo)
            new_hi = jnp.where(z_hi == 1, moved_z // 2, other_hi)
        new_core = lax.rem(self.core + core, 2) if mix else self.core
        return self.index(new_lo, new_core, new_y, new_x, new_hi)


def far(flip):
    z_lo, _, y, x, z_hi = flip
    if y == 2:
        return True
    return (x == 2) if z_lo else jnp.logical_or(x == 2, z_hi == 1)


def both(first, second):
    return {"tm": first, "inp": second}


def when(condition, action):
    if condition is True:
        action()
    else:
        pl.when(condition)(action)


def each_flip(action):
    @pl.loop(0, 8)
    def _(outer):
        x, z_hi = lax.rem(outer, 4), outer // 4
        for inner in range(16):
            flip = (inner % 2, (inner // 2) % 2, inner // 4, x, z_hi)
            if inner == 0:
                pl.when(outer > 0)(functools.partial(action, flip))
            else:
                action(flip)


def spread_spectra(
    frames, fine, history, volt, taps, low_cos, low_sin, high_cos, high_sin, out,
    samples, filtered, stage, relay, table, wide_taps, in_sem, give_sem, send_sem, relay_sem, pass_sem, recv_sem, own_sem,
):
    place = Place()
    me = lax.axis_index("tm") * 2 + lax.axis_index("inp")
    core = place.core
    partner = lax.axis_index("tm") + 1 - 2 * core
    span = 2 * frames
    produced = span + history
    half = samples.shape[3]
    devices = stage.shape[0]
    barrier = pltpu.get_barrier_semaphore()

    def greet(flip):
        pl.semaphore_signal(barrier, inc=1, device_id=both(*place.flipped(flip)), device_id_type=MESH)

    each_flip(greet)

    def lanes(which):
        return pl.ds(pl.multiple_of(which * half, half), half)

    order = [(f, r) for f in range(frames) for r in range(2)]
    for f, r in order:
        source = volt.at[r, pl.ds(f * fine, fine), lanes(core)]
        pltpu.make_async_copy(source, samples.at[core * frames + f, r], in_sem.at[core * frames + f, r]).start()

    rows = 16

    @pl.loop(0, fine // rows)
    def _(step):
        at = pl.ds(pl.multiple_of(step * rows, rows), rows)
        tap_rows = taps[at, :]
        for k in range(history + 1):
            wide_taps[k, at] = jnp.broadcast_to(tap_rows[:, k : k + 1], (rows, 128))

    @pl.loop(0, table.shape[0] // rows)
    def _(step):
        at = pl.ds(pl.multiple_of(step * rows, rows), rows)
        base_cos, base_sin = low_cos[at, :], low_sin[at, :]
        more_cos, more_sin = high_cos[at, :], high_sin[at, :]
        for block in range(fine // 128):
            turn_cos = jnp.broadcast_to(more_cos[:, block : block + 1], (rows, 128))
            turn_sin = jnp.broadcast_to(more_sin[:, block : block + 1], (rows, 128))
            table[at, pl.ds(block * 128, 128)] = (turn_cos * base_cos - turn_sin * base_sin).astype(jnp.bfloat16)
            table[at, pl.ds(fine + block * 128, 128)] = (turn_sin * base_cos + turn_cos * base_sin).astype(jnp.bfloat16)

    pl.semaphore_wait(barrier, devices - 1)

    given = []
    for f, r in order:
        given.append(
            pltpu.make_async_remote_copy(
                src_ref=volt.at[r, pl.ds(f * fine, fine), lanes(1 - core)],
                dst_ref=samples.at[core * frames + f, r],
                send_sem=give_sem.at[f, r],
                recv_sem=in_sem.at[core * frames + f, r],
                device_id={"tm": partner},
                device_id_type=MESH,
            )
        )
        given[-1].start()

    def send(chunk, piece, flip):
        first, second = place.flipped(flip)

        def straight():
            pltpu.make_async_remote_copy(
                src_ref=stage.at[first * 2 + second, piece],
                dst_ref=out.at[me, piece],
                send_sem=send_sem,
                recv_sem=recv_sem,
                device_id=both(first, second),
                device_id_type=MESH,
            ).start()

        def relayed():
            z_lo, _, y, x, z_hi = flip
            pltpu.make_async_remote_copy(
                src_ref=stage.at[first * 2 + second, piece],
                dst_ref=relay.at[((z_hi * 4 + x) * 4 + y) * 2 + z_lo, piece],
                send_sem=send_sem,
                recv_sem=relay_sem.at[chunk],
                device_id=both(*place.shifted(flip, STEP_BACK, False)),
                device_id_type=MESH,
            ).start()

        if flip[1] == 0:
            straight()
        else:
            is_far = far(flip)
            when(is_far, relayed)
            if is_far is not True:
                pl.when(jnp.logical_not(is_far))(straight)

    def pass_on(chunk, piece):
        waited = relay.at[pl.ds(0, 37), piece]
        pltpu.make_async_copy(waited, waited, relay_sem.at[chunk]).wait()

        def forward(flip):
            if flip[1] == 0:
                return
            z_lo, _, y, x, z_hi = flip
            came_time, came_lo = place.shifted(flip, 4 - STEP_BACK, False)

            def go():
                pltpu.make_async_remote_copy(
                    src_ref=relay.at[((z_hi * 4 + x) * 4 + y) * 2 + z_lo, piece],
                    dst_ref=out.at[came_time * 2 + came_lo, piece],
                    send_sem=pass_sem,
                    recv_sem=recv_sem,
                    device_id=both(*place.shifted(flip, STEP_BACK, True)),
                    device_id_type=MESH,
                ).start()

            when(far(flip), go)

        each_flip(forward)

    begin = 0
    pieces = []
    arrived = 0
    for chunk, count in enumerate(CHUNKS):
        end = begin + count
        while arrived < min(span, end):
            for r in range(2):
                pltpu.make_async_copy(samples.at[arrived, r], samples.at[arrived, r], in_sem.at[arrived, r]).wait()
            arrived += 1
        inputs = [i for i in range(span) if begin - history <= i < end]

        @pl.loop(0, fine // rows)
        def _(step):
            at = pl.ds(pl.multiple_of(step * rows, rows), rows)
            for r in range(2):
                for lane in range(half // 128):
                    cols = pl.ds(lane * 128, 128)
                    held = {i: samples[i, r, at, cols].astype(jnp.float32) for i in inputs}
                    for f in range(begin, end):
                        total = None
                        for i in inputs:
                            if 0 <= f - i <= history:
                                term = wide_taps[f - i, at] * held[i]
                                total = term if total is None else total + term
                        filtered[f - begin, pl.ds(pl.multiple_of(r * fine + step * rows, rows), rows), cols] = total.astype(jnp.bfloat16)

        @pl.loop(0, count)
        def _(f):
            product = jnp.dot(table[...], filtered[f], preferred_element_type=jnp.float32)
            stage[:, begin + f] = product.astype(jnp.bfloat16).reshape(devices, stage.shape[2], half)

        piece = pl.ds(begin, count)
        pieces.append(piece)
        each_flip(functools.partial(send, chunk, piece))
        if chunk >= 1:
            pass_on(chunk - 1, pieces[chunk - 1])
        begin = end

    own = pltpu.make_async_copy(stage.at[me], out.at[me], own_sem)
    own.start()
    pass_on(len(CHUNKS) - 1, pieces[-1])
    own.wait()
    for copy in given:
        copy.wait_send()
    sent = stage.at[pl.ds(0, devices - 1)]
    pltpu.make_async_copy(sent, sent, send_sem).wait()
    passed = relay.at[pl.ds(0, 37)]
    pltpu.make_async_copy(passed, passed, pass_sem).wait()
    taken = out.at[pl.ds(0, devices - 1)]
    pltpu.make_async_copy(taken, taken, recv_sem).wait()


def correlate(chips, span, history, inverse, received, out, turned_in, spectra, wide):
    width = received.shape[-1]
    groups = received.shape[1]
    total_inputs = groups * width
    frames = chips * span

    @pl.when(pl.program_id(0) == 0)
    def _():
        @pl.loop(0, chips // 2)
        def _(pair):
            for group in range(groups):
                column = (group % 2) * 2 + group // 2
                for lane in range(width // 128):
                    cols = pl.ds(lane * 128, 128)
                    for sub in range(2):
                        chip = pair * 2 + sub
                        for i in range(span):
                            value = received[chip, group, i, :, cols].astype(jnp.float32)
                            back = 1
                            while i + back * span < span + history:
                                earlier = received[jnp.maximum(chip - back, 0), group, i + back * span, :, cols].astype(jnp.float32)
                                value = value + jnp.where(chip >= back, earlier, 0.0)
                                back += 1
                            wide[pl.ds((sub * span + i) * 8, 8), :] = value
                    for row in range(8):
                        picked = wide[pl.ds(row, 2 * span, stride=8), :].astype(jnp.bfloat16)
                        here = pl.ds(pl.multiple_of((row % 2) * frames + pair * (2 * span), 2 * span), 2 * span)
                        there = pl.ds(pl.multiple_of((1 - row % 2) * frames + pair * (2 * span), 2 * span), 2 * span)
                        at = pl.ds(column * width + lane * 128, 128)
                        spectra[row // 2, here, at] = picked
                        turned_in[row // 2, there, at] = -picked if row % 2 else picked

    chan = pl.program_id(0)
    upper = lax.broadcasted_iota(jnp.int32, (width, width), 0) <= lax.broadcasted_iota(jnp.int32, (width, width), 1)
    contract = (((0,), (0,)), ((), ()))
    for a in range(total_inputs // width):
        rows = pl.ds(a * width, width)
        left = spectra[chan, :, rows]
        real = lax.dot_general(left, spectra[chan, :, pl.ds(a * width, total_inputs - a * width)], contract, preferred_element_type=jnp.float32)
        imag = lax.dot_general(left, turned_in[chan, :, pl.ds(0, (a + 1) * width)], contract, preferred_element_type=jnp.float32)
        if a:
            out[0, rows, pl.ds(0, a * width)] = (imag[:, : a * width] * inverse).astype(jnp.bfloat16)
        middle = jnp.where(upper, real[:, :width], imag[:, a * width :])
        out[0, rows, pl.ds(a * width, width)] = (middle * inverse).astype(jnp.bfloat16)
        if (a + 1) * width < total_inputs:
            out[0, rows, pl.ds((a + 1) * width, total_inputs - (a + 1) * width)] = (real[:, width:] * inverse).astype(jnp.bfloat16)


def per_device(voltages, taps):
    history = taps.shape[0] - 1
    fine = taps.shape[1]
    frames = voltages.shape[1] // fine
    width = voltages.shape[2]
    n_time = lax.axis_size("tm")
    n_group = lax.axis_size("inp")
    devices = n_time * n_group
    chans = KEEP // devices
    half = width // 2
    span = 2 * frames
    produced = span + history
    chips = n_time // 2
    scaled = (taps.astype(jnp.float32) * (1.0 / 8192.0)).T
    tables = [jnp.asarray(x) for x in table_parts(fine, KEEP)]
    vmem = pl.BlockSpec(memory_space=pltpu.VMEM)
    hbm = pl.BlockSpec(memory_space=pl.ANY)
    moved = pl.pallas_call(
        functools.partial(spread_spectra, frames, fine, history),
        out_shape=jax.ShapeDtypeStruct((devices, produced, 2 * chans, half), jnp.bfloat16),
        in_specs=[hbm] + [vmem] * 5,
        out_specs=hbm,
        scratch_shapes=[
            pltpu.VMEM((span, 2, fine, half), jnp.bfloat16),
            pltpu.VMEM((max(CHUNKS), 2 * fine, half), jnp.bfloat16),
            pltpu.VMEM((devices, produced, 2 * chans, half), jnp.bfloat16),
            pltpu.VMEM((devices // 2, produced, 2 * chans, half), jnp.bfloat16),
            pltpu.VMEM((2 * KEEP, 2 * fine), jnp.bfloat16),
            pltpu.VMEM((history + 1, fine, 128), jnp.float32),
            pltpu.SemaphoreType.DMA((span, 2)),
            pltpu.SemaphoreType.DMA((frames, 2)),
            pltpu.SemaphoreType.DMA,
            pltpu.SemaphoreType.DMA((len(CHUNKS),)),
            pltpu.SemaphoreType.DMA,
            pltpu.SemaphoreType.DMA,
            pltpu.SemaphoreType.DMA,
        ],
        compiler_params=pltpu.CompilerParams(collective_id=0, has_side_effects=True, vmem_limit_bytes=58 * 2**20),
        name="spread_spectra",
    )(voltages, scaled, *tables)
    received = moved.reshape(chips, 2 * n_group, produced, 2 * chans, half)
    total = width * n_group
    return pl.pallas_call(
        functools.partial(correlate, chips, span, history, 1.0 / (chips * span)),
        out_shape=jax.ShapeDtypeStruct((chans, total, total), jnp.bfloat16),
        grid=(chans,),
        in_specs=[pl.BlockSpec(memory_space=pltpu.VMEM)],
        out_specs=pl.BlockSpec((1, total, total), lambda c: (c, 0, 0)),
        scratch_shapes=[
            pltpu.VMEM((chans, 2 * chips * span, total), jnp.bfloat16),
            pltpu.VMEM((chans, 2 * chips * span, total), jnp.bfloat16),
            pltpu.VMEM((2 * span * 8, 128), jnp.float32),
        ],
        compiler_params=pltpu.CompilerParams(vmem_limit_bytes=56 * 2**20),
        name="correlate",
    )(received)


def solution(mesh):
    placed = (P(None, "tm", "inp"), P())
    return jax.shard_map(
        per_device,
        mesh=mesh,
        in_specs=placed,
        out_specs=P(("tm", "inp"), None, None),
        check_vma=False,
    )
```

```python
import functools
import math

import jax
import jax.numpy as jnp
import numpy as np
from jax import lax
from jax.experimental import pallas as pl
from jax.experimental.pallas import tpu as pltpu
from jax.sharding import PartitionSpec as P

KEEP = 512
MESH = pl.DeviceIdType.MESH


UNITS = ((0, 1, 2), (8, 16), (9, 17), (10, 18), (3, 11), (4, 12), (5, 13), (6, 14), (7, 15))
RING = 4


def table_parts(fine, keep, owned):
    chan = (np.arange(keep) - keep // 2).reshape(-1, RING, 4 * owned)
    chan = np.repeat(chan.transpose(1, 0, 2).reshape(-1), 2)
    part = np.tile(np.arange(2), keep)
    low = (chan[:, None] * np.arange(128)[None, :] + part[:, None] * (fine // 4)) % fine
    high = (chan[:, None] * np.arange(0, fine, 128)[None, :]) % fine
    scale = 1.0 / math.sqrt(fine)
    step = 2.0 * np.pi / fine
    return tuple(
        x.astype(np.float32)
        for x in (np.cos(step * low) * scale, np.sin(step * low) * scale, np.cos(step * high), np.sin(step * high))
    )


def row_slots(span, history):
    slots, count = {}, 0
    for q in range(span):
        for m in range(RING + (history + span - 1 - q) // span):
            slots[q, m] = count
            count += 1
    return slots, count


class Place:
    def __init__(self):
        time, self.z_lo = lax.axis_index("tm"), lax.axis_index("inp")
        self.core, self.y = lax.rem(time, 2), lax.rem(time // 2, RING)
        self.x, self.z_hi = lax.rem(time // 8, 4), time // 32

    def device(self, y, x, z_hi, core, z_lo):
        return {"tm": ((z_hi * 4 + x) * RING + y) * 2 + core, "inp": z_lo}

    def along(self, steps):
        return self.device(lax.rem(self.y + steps + RING, RING), self.x, self.z_hi, self.core, self.z_lo)

    def flipped(self, flip):
        x_flip, z_hi_flip, core_flip, z_lo_flip = flip
        x = lax.rem(self.x // 2 + x_flip // 2, 2) * 2 + lax.rem(self.x + x_flip, 2)
        z_hi = lax.rem(self.z_hi + z_hi_flip, 2)
        core, z_lo = lax.rem(self.core + core_flip, 2), lax.rem(self.z_lo + z_lo_flip, 2)
        return self.device(self.y, x, z_hi, core, z_lo), ((z_hi * 4 + x) * 2 + core) * 2 + z_lo

    def number(self):
        return ((self.z_hi * 4 + self.x) * 2 + self.core) * 2 + self.z_lo


def each_flip(action):
    @pl.loop(0, 8)
    def _(outer):
        for inner in range(4):
            flip = (lax.rem(outer, 4), outer // 4, inner % 2, inner // 2)
            if inner == 0:
                pl.when(outer > 0)(functools.partial(action, flip))
            else:
                action(flip)


def spread_spectra(
    frames, fine, history, volt, taps, low_cos, low_sin, high_cos, high_sin, out,
    samples, filtered, stage, heard, relay, summed, table, wide_taps,
    in_sem, give_sem, send_sem, relay_sem, pass_sem, heard_sem, keep_sem, plane_sem, recv_sem, own_sem,
):
    place = Place()
    core, here = place.core, place.number()
    partner = lax.axis_index("tm") + 1 - 2 * core
    span = 2 * frames
    half = samples.shape[3]
    plane = summed.shape[0]
    slots, _ = row_slots(span, history)
    order = [f for unit in UNITS for f in unit]
    slot_of = {f: i for i, f in enumerate(order)}
    barrier = pltpu.get_barrier_semaphore()

    def greet(flip):
        pl.semaphore_signal(barrier, inc=1, device_id=place.flipped(flip)[0], device_id_type=MESH)

    each_flip(greet)
    for steps in (1, -1):
        pl.semaphore_signal(barrier, inc=1, device_id=place.along(steps), device_id_type=MESH)

    def lanes(which):
        return pl.ds(pl.multiple_of(which * half, half), half)

    pieces = [(f, r) for f in range(frames) for r in range(2)]
    for f, r in pieces:
        source = volt.at[r, pl.ds(f * fine, fine), lanes(core)]
        pltpu.make_async_copy(source, samples.at[core * frames + f, r], in_sem.at[core * frames + f, r]).start()

    rows = 16

    @pl.loop(0, fine // rows)
    def _(step):
        at = pl.ds(pl.multiple_of(step * rows, rows), rows)
        tap_rows = taps[at, :]
        for k in range(history + 1):
            wide_taps[k, at] = jnp.broadcast_to(tap_rows[:, k : k + 1], (rows, 128))

    pl.semaphore_wait(barrier, plane + 1)

    given = []
    for f, r in pieces:
        given.append(
            pltpu.make_async_remote_copy(
                src_ref=volt.at[r, pl.ds(f * fine, fine), lanes(1 - core)],
                dst_ref=samples.at[core * frames + f, r],
                send_sem=give_sem.at[f, r],
                recv_sem=in_sem.at[core * frames + f, r],
                device_id={"tm": partner},
                device_id_type=MESH,
            )
        )
        given[-1].start()

    @pl.loop(0, table.shape[0] // rows)
    def _(step):
        at = pl.ds(pl.multiple_of(step * rows, rows), rows)
        base_cos, base_sin = low_cos[at, :], low_sin[at, :]
        more_cos, more_sin = high_cos[at, :], high_sin[at, :]
        for block in range(fine // 128):
            turn_cos = jnp.broadcast_to(more_cos[:, block : block + 1], (rows, 128))
            turn_sin = jnp.broadcast_to(more_sin[:, block : block + 1], (rows, 128))
            table[at, pl.ds(block * 128, 128)] = (turn_cos * base_cos - turn_sin * base_sin).astype(jnp.bfloat16)
            table[at, pl.ds(fine + block * 128, 128)] = (turn_sin * base_cos + turn_cos * base_sin).astype(jnp.bfloat16)

    def remote(source, target, send, recv, device):
        pltpu.make_async_remote_copy(
            src_ref=source, dst_ref=target, send_sem=send, recv_sem=recv, device_id=device, device_id_type=MESH
        ).start()

    hops = ((0, 1), (1, -1))

    def half_of(side):
        return pl.ds(side * (plane // 2), plane // 2)

    def send(unit, at):
        across = lax.rem(place.y + 2, RING)
        for side, steps in hops:
            remote(stage.at[at, across, half_of(side)], relay.at[at, side], send_sem, relay_sem.at[unit], place.along(steps))
        for side, steps in hops:
            to = lax.rem(place.y + steps + RING, RING)
            remote(stage.at[at, to], heard.at[at, place.y], send_sem, heard_sem.at[unit], place.along(steps))
        pltpu.make_async_copy(stage.at[at, place.y], heard.at[at, place.y], keep_sem.at[unit]).start()

    def pass_on(unit, at):
        pltpu.make_async_copy(relay.at[at], relay.at[at], relay_sem.at[unit]).wait()
        for side, steps in hops:
            came = lax.rem(place.y - steps + RING, RING)
            remote(relay.at[at, side], heard.at[at, came, half_of(side)], pass_sem, heard_sem.at[unit], place.along(steps))

    def hear(unit, at):
        three = heard.at[at, pl.ds(0, RING - 1)]
        pltpu.make_async_copy(three, three, heard_sem.at[unit]).wait()
        one = heard.at[at, 0]
        pltpu.make_async_copy(one, one, keep_sem.at[unit]).wait()

    def finish(q):
        ms = [m for (other, m) in slots if other == q]
        locals_ = [f for f in range(q, span + history, span)]

        @pl.loop(0, plane)
        def _(device):
            for m in ms:
                total = None
                for j, f in enumerate(locals_):
                    if 0 <= m - j < RING:
                        term = heard[slot_of[f], m - j, device].astype(jnp.float32)
                        total = term if total is None else total + term
                summed[device, slots[q, m]] = total.astype(jnp.bfloat16)

        piece = pl.ds(slots[q, 0], len(ms))

        def spread(flip):
            device, number = place.flipped(flip)
            remote(summed.at[number, piece], out.at[here, piece], plane_sem, recv_sem, device)

        each_flip(spread)

    at = []
    begin = 0
    arrived = 0
    for unit, outputs in enumerate(UNITS):
        count = len(outputs)
        while arrived <= min(span - 1, max(outputs)):
            for r in range(2):
                pltpu.make_async_copy(samples.at[arrived, r], samples.at[arrived, r], in_sem.at[arrived, r]).wait()
            arrived += 1
        inputs = [i for i in range(span) if any(0 <= f - i <= history for f in outputs)]

        @pl.loop(0, fine // rows)
        def _(step):
            here_rows = pl.ds(pl.multiple_of(step * rows, rows), rows)
            for r in range(2):
                for lane in range(half // 128):
                    cols = pl.ds(lane * 128, 128)
                    held = {i: samples[i, r, here_rows, cols].astype(jnp.float32) for i in inputs}
                    for place_in, f in enumerate(outputs):
                        total = None
                        for i in inputs:
                            if 0 <= f - i <= history:
                                term = wide_taps[f - i, here_rows] * held[i]
                                total = term if total is None else total + term
                        filtered[place_in, pl.ds(pl.multiple_of(r * fine + step * rows, rows), rows), cols] = total.astype(jnp.bfloat16)

        @pl.loop(0, count)
        def _(f):
            product = jnp.dot(table[...], filtered[f], preferred_element_type=jnp.float32)
            stage[begin + f] = product.astype(jnp.bfloat16).reshape(stage.shape[1:])

        at.append(pl.ds(begin, count))
        send(unit, at[unit])
        if unit >= 1:
            pass_on(unit - 1, at[unit - 1])
        if unit >= 2:
            hear(unit - 2, at[unit - 2])
        if unit >= 3:
            finish(UNITS[unit - 2][0] % span)
        begin += count

    last = len(UNITS) - 1
    pass_on(last, at[last])
    for unit in (last - 1, last):
        hear(unit, at[unit])
        finish(UNITS[unit][0] % span)
    own = pltpu.make_async_copy(summed.at[here], out.at[here], own_sem)
    own.start()
    own.wait()
    for copy in given:
        copy.wait_send()
    sent = stage.at[:, pl.ds(0, RING - 1)]
    pltpu.make_async_copy(sent, sent, send_sem).wait()
    pltpu.make_async_copy(relay, relay, pass_sem).wait()
    others = summed.at[pl.ds(0, plane - 1)]
    pltpu.make_async_copy(others, others, plane_sem).wait()
    taken = out.at[pl.ds(0, plane - 1)]
    pltpu.make_async_copy(taken, taken, recv_sem).wait()


def correlate(span, history, inverse, received, out, turned_in, spectra, wide):
    lines, groups = received.shape[:2]
    width = received.shape[-1]
    total_inputs = groups * width
    frames = lines * RING * span
    slots, _ = row_slots(span, history)

    @pl.when(pl.program_id(0) == 0)
    def _():
        @pl.loop(0, lines)
        def _(line):
            for pair in range(RING // 2):
                for group in range(groups):
                    column = (group % 2) * 2 + group // 2
                    for lane in range(width // 128):
                        cols = pl.ds(lane * 128, 128)
                        for sub in range(2):
                            m = pair * 2 + sub
                            for q in range(span):
                                value = received[line, group, slots[q, m], :, cols].astype(jnp.float32)
                                if (q, m + RING) in slots:
                                    earlier = received[jnp.maximum(line - 1, 0), group, slots[q, m + RING], :, cols]
                                    value = value + jnp.where(line > 0, earlier.astype(jnp.float32), 0.0)
                                wide[pl.ds((sub * span + q) * 8, 8), :] = value
                        for row in range(8):
                            picked = wide[pl.ds(row, 2 * span, stride=8), :].astype(jnp.bfloat16)
                            first = line * (RING * span) + pair * 2 * span
                            here = pl.ds(pl.multiple_of((row % 2) * frames + first, 2 * span), 2 * span)
                            there = pl.ds(pl.multiple_of((1 - row % 2) * frames + first, 2 * span), 2 * span)
                            at = pl.ds(column * width + lane * 128, 128)
                            spectra[row // 2, here, at] = picked
                            turned_in[row // 2, there, at] = -picked if row % 2 else picked

    chan = pl.program_id(0)
    upper = lax.broadcasted_iota(jnp.int32, (width, width), 0) <= lax.broadcasted_iota(jnp.int32, (width, width), 1)
    contract = (((0,), (0,)), ((), ()))
    for a in range(total_inputs // width):
        rows = pl.ds(a * width, width)
        left = spectra[chan, :, rows]
        real = lax.dot_general(left, spectra[chan, :, pl.ds(a * width, total_inputs - a * width)], contract, preferred_element_type=jnp.float32)
        imag = lax.dot_general(left, turned_in[chan, :, pl.ds(0, (a + 1) * width)], contract, preferred_element_type=jnp.float32)
        if a:
            out[0, rows, pl.ds(0, a * width)] = (imag[:, : a * width] * inverse).astype(jnp.bfloat16)
        middle = jnp.where(upper, real[:, :width], imag[:, a * width :])
        out[0, rows, pl.ds(a * width, width)] = (middle * inverse).astype(jnp.bfloat16)
        if (a + 1) * width < total_inputs:
            out[0, rows, pl.ds((a + 1) * width, total_inputs - (a + 1) * width)] = (real[:, width:] * inverse).astype(jnp.bfloat16)


def per_device(voltages, taps):
    history = taps.shape[0] - 1
    fine = taps.shape[1]
    frames = voltages.shape[1] // fine
    width = voltages.shape[2]
    n_time = lax.axis_size("tm")
    n_group = lax.axis_size("inp")
    devices = n_time * n_group
    chans = KEEP // devices
    half = width // 2
    span = 2 * frames
    produced = span + history
    plane = devices // RING
    lines = plane // 4
    rows_kept = row_slots(span, history)[1]
    scaled = (taps.astype(jnp.float32) * (1.0 / 8192.0)).T
    tables = [jnp.asarray(x) for x in table_parts(fine, KEEP, chans)]
    vmem = pl.BlockSpec(memory_space=pltpu.VMEM)
    hbm = pl.BlockSpec(memory_space=pl.ANY)
    block = (2 * chans, half)
    biggest = max(len(unit) for unit in UNITS)
    moved = pl.pallas_call(
        functools.partial(spread_spectra, frames, fine, history),
        out_shape=jax.ShapeDtypeStruct((plane, rows_kept, *block), jnp.bfloat16),
        in_specs=[hbm] + [vmem] * 5,
        out_specs=hbm,
        scratch_shapes=[
            pltpu.VMEM((span, 2, fine, half), jnp.bfloat16),
            pltpu.VMEM((biggest, 2 * fine, half), jnp.bfloat16),
            pltpu.VMEM((produced, RING, plane, *block), jnp.bfloat16),
            pltpu.VMEM((produced, RING, plane, *block), jnp.bfloat16),
            pltpu.VMEM((produced, 2, plane // 2, *block), jnp.bfloat16),
            pltpu.VMEM((plane, rows_kept, *block), jnp.bfloat16),
            pltpu.VMEM((2 * KEEP, 2 * fine), jnp.bfloat16),
            pltpu.VMEM((history + 1, fine, 128), jnp.float32),
            pltpu.SemaphoreType.DMA((span, 2)),
            pltpu.SemaphoreType.DMA((frames, 2)),
            pltpu.SemaphoreType.DMA,
            pltpu.SemaphoreType.DMA((len(UNITS),)),
            pltpu.SemaphoreType.DMA,
            pltpu.SemaphoreType.DMA((len(UNITS),)),
            pltpu.SemaphoreType.DMA((len(UNITS),)),
            pltpu.SemaphoreType.DMA,
            pltpu.SemaphoreType.DMA,
            pltpu.SemaphoreType.DMA,
        ],
        compiler_params=pltpu.CompilerParams(collective_id=0, has_side_effects=True, vmem_limit_bytes=60 * 2**20),
        name="spread_spectra",
    )(voltages, scaled, *tables)
    received = moved.reshape(lines, 2 * n_group, rows_kept, *block)
    total = width * n_group
    return pl.pallas_call(
        functools.partial(correlate, span, history, 1.0 / (n_time * frames)),
        out_shape=jax.ShapeDtypeStruct((chans, total, total), jnp.bfloat16),
        grid=(chans,),
        in_specs=[pl.BlockSpec(memory_space=pltpu.VMEM)],
        out_specs=pl.BlockSpec((1, total, total), lambda c: (c, 0, 0)),
        scratch_shapes=[
            pltpu.VMEM((chans, 2 * n_time * frames, total), jnp.bfloat16),
            pltpu.VMEM((chans, 2 * n_time * frames, total), jnp.bfloat16),
            pltpu.VMEM((2 * span * 8, 128), jnp.float32),
        ],
        compiler_params=pltpu.CompilerParams(vmem_limit_bytes=56 * 2**20),
        name="correlate",
    )(received)


def solution(mesh):
    placed = (P(None, "tm", "inp"), P())
    return jax.shard_map(
        per_device,
        mesh=mesh,
        in_specs=placed,
        out_specs=P(("tm", "inp"), None, None),
        check_vma=False,
    )
```

```python
import functools
import math

import jax
import jax.numpy as jnp
import numpy as np
from jax import lax
from jax.experimental import pallas as pl
from jax.experimental.pallas import tpu as pltpu
from jax.sharding import PartitionSpec as P

KEEP = 512
MESH = pl.DeviceIdType.MESH


UNITS = ((0,), (1, 2), (8, 16), (9, 17), (10, 18), (3, 11), (4, 12), (5, 13), (6, 14), (7, 15))
FIRST_SUM = 2
RING = 4


def table_parts(fine, keep, owned):
    chan = (np.arange(keep) - keep // 2).reshape(-1, RING, 2, 2 * owned)
    chan = np.repeat(chan.transpose(1, 2, 0, 3).reshape(-1), 2)
    part = np.tile(np.arange(2), keep)
    low = (chan[:, None] * np.arange(128)[None, :] + part[:, None] * (fine // 4)) % fine
    high = (chan[:, None] * np.arange(0, fine, 128)[None, :]) % fine
    scale = 1.0 / math.sqrt(fine)
    step = 2.0 * np.pi / fine
    return tuple(
        x.astype(np.float32)
        for x in (np.cos(step * low) * scale, np.sin(step * low) * scale, np.cos(step * high), np.sin(step * high))
    )


def row_slots(span, history):
    slots, count = {}, 0
    for q in range(span):
        for m in range(RING + (history + span - 1 - q) // span):
            slots[q, m] = count
            count += 1
    return slots, count


class Place:
    def __init__(self):
        time, self.z_lo = lax.axis_index("tm"), lax.axis_index("inp")
        self.core, self.y = lax.rem(time, 2), lax.rem(time // 2, RING)
        self.x, self.z_hi = lax.rem(time // 8, 4), time // 32

    def device(self, y, x, z_hi, core, z_lo):
        return {"tm": ((z_hi * 4 + x) * RING + y) * 2 + core, "inp": z_lo}

    def along(self, steps):
        return self.device(lax.rem(self.y + steps + RING, RING), self.x, self.z_hi, self.core, self.z_lo)

    def flipped(self, flip):
        x_flip, z_hi_flip, core_flip, z_lo_flip = flip
        x = lax.rem(self.x // 2 + x_flip // 2, 2) * 2 + lax.rem(self.x + x_flip, 2)
        z_hi = lax.rem(self.z_hi + z_hi_flip, 2)
        core, z_lo = lax.rem(self.core + core_flip, 2), lax.rem(self.z_lo + z_lo_flip, 2)
        return self.device(self.y, x, z_hi, core, z_lo), ((core * 2 + z_hi) * 4 + x) * 2 + z_lo

    def number(self):
        return ((self.core * 2 + self.z_hi) * 4 + self.x) * 2 + self.z_lo

    def each_other(self, core, action):
        core_flip = lax.rem(self.core + core, 2)

        @pl.loop(0, 8)
        def _(outer):
            for z_lo_flip in range(2):
                flip = (lax.rem(outer, 4), outer // 4, core_flip, z_lo_flip)
                if z_lo_flip:
                    action(flip)
                else:
                    pl.when(outer + core_flip > 0)(functools.partial(action, flip))


def spread_spectra(
    frames, fine, history, volt, taps, low_cos, low_sin, high_cos, high_sin, out,
    samples, filtered, stage, heard, relay, summed, received, spectra, turning, table, wide_taps,
    in_sem, give_sem, send_sem, relay_sem, pass_sem, heard_sem, keep_sem, plane_sem, recv_sem, own_sem, out_sem,
):
    place = Place()
    core, here = place.core, place.number()
    partner = lax.axis_index("tm") + 1 - 2 * core
    span = 2 * frames
    half = samples.shape[3]
    plane = summed.shape[0]
    slots, _ = row_slots(span, history)
    order = [f for unit in UNITS for f in unit]
    slot_of = {f: i for i, f in enumerate(order)}
    barrier = pltpu.get_barrier_semaphore()

    def greet(flip):
        pl.semaphore_signal(barrier, inc=1, device_id=place.flipped(flip)[0], device_id_type=MESH)

    for which in range(2):
        place.each_other(which, greet)
    for steps in (1, -1):
        pl.semaphore_signal(barrier, inc=1, device_id=place.along(steps), device_id_type=MESH)

    def lanes(which):
        return pl.ds(pl.multiple_of(which * half, half), half)

    pieces = [(f, r) for f in range(frames) for r in range(2)]
    for f, r in pieces:
        source = volt.at[r, pl.ds(f * fine, fine), lanes(core)]
        pltpu.make_async_copy(source, samples.at[core * frames + f, r], in_sem.at[core * frames + f, r]).start()

    rows = 16

    @pl.loop(0, fine // rows)
    def _(step):
        at = pl.ds(pl.multiple_of(step * rows, rows), rows)
        tap_rows = taps[at, :].astype(jnp.float32) * (1.0 / 8192.0)
        for k in range(history + 1):
            wide_taps[k, at] = jnp.broadcast_to(tap_rows[:, k : k + 1], (rows, 128))

    pl.semaphore_wait(barrier, plane + 1)

    given = []
    for f, r in pieces:
        given.append(
            pltpu.make_async_remote_copy(
                src_ref=volt.at[r, pl.ds(f * fine, fine), lanes(1 - core)],
                dst_ref=samples.at[core * frames + f, r],
                send_sem=give_sem.at[f, r],
                recv_sem=in_sem.at[core * frames + f, r],
                device_id={"tm": partner},
                device_id_type=MESH,
            )
        )
        given[-1].start()

    @pl.loop(0, table.shape[0] // rows)
    def _(step):
        at = pl.ds(pl.multiple_of(step * rows, rows), rows)
        base_cos, base_sin = low_cos[at, :], low_sin[at, :]
        more_cos, more_sin = high_cos[at, :], high_sin[at, :]
        for block in range(fine // 128):
            turn_cos = jnp.broadcast_to(more_cos[:, block : block + 1], (rows, 128))
            turn_sin = jnp.broadcast_to(more_sin[:, block : block + 1], (rows, 128))
            table[at, pl.ds(block * 128, 128)] = (turn_cos * base_cos - turn_sin * base_sin).astype(jnp.bfloat16)
            table[at, pl.ds(fine + block * 128, 128)] = (turn_sin * base_cos + turn_cos * base_sin).astype(jnp.bfloat16)

    def remote(source, target, send, recv, device):
        pltpu.make_async_remote_copy(
            src_ref=source, dst_ref=target, send_sem=send, recv_sem=recv, device_id=device, device_id_type=MESH
        ).start()

    hops = ((0, 1), (1, -1))

    last = len(UNITS) - 1
    loads = [(unit, 0, plane) for unit in range(last)] + [(last, which * (plane // 2), plane // 2) for which in range(2)]

    def half_of(load, side):
        _, first, size = loads[load]
        return pl.ds(first + side * (size // 2), size // 2)

    def relayed(load):
        _, first, size = loads[load]
        return pl.ds(first // 2, size // 2)

    def send(load):
        unit, first, size = loads[load]
        across = lax.rem(place.y + 2, RING)
        whole = pl.ds(first, size)
        for side, steps in hops:
            remote(stage.at[at[unit], across, half_of(load, side)], relay.at[at[unit], side, relayed(load)], send_sem, relay_sem.at[load], place.along(steps))
        for side, steps in hops:
            to = lax.rem(place.y + steps + RING, RING)
            remote(stage.at[at[unit], to, whole], heard.at[at[unit], place.y, whole], send_sem, heard_sem.at[load], place.along(steps))
        pltpu.make_async_copy(stage.at[at[unit], place.y, whole], heard.at[at[unit], place.y, whole], keep_sem.at[load]).start()

    def pass_on(load):
        unit = loads[load][0]
        came_in = relay.at[at[unit], :, relayed(load)]
        pltpu.make_async_copy(came_in, came_in, relay_sem.at[load]).wait()
        for side, steps in hops:
            came = lax.rem(place.y - steps + RING, RING)
            remote(
                relay.at[at[unit], side, relayed(load)], heard.at[at[unit], came, half_of(load, side)], pass_sem, heard_sem.at[load], place.along(steps)
            )

    done = set()

    def finish(load):
        unit, first, size = loads[load]
        whole = pl.ds(first, size)
        three = heard.at[at[unit], pl.ds(0, RING - 1), whole]
        pltpu.make_async_copy(three, three, heard_sem.at[load]).wait()
        one = heard.at[at[unit], 0, whole]
        pltpu.make_async_copy(one, one, keep_sem.at[load]).wait()
        if unit < FIRST_SUM:
            return
        q = UNITS[unit][0] % span
        ms = [m for (other, m) in slots if other == q]
        parts = list(range(q, span + history, span))

        @pl.loop(first, first + size)
        def _(device):
            for m in ms:
                total = None
                for j, f in enumerate(parts):
                    if 0 <= m - j < RING:
                        term = heard[slot_of[f], m - j, device].astype(jnp.float32)
                        total = term if total is None else total + term
                summed[device, slots[q, m]] = total.astype(jnp.bfloat16)

        piece = pl.ds(slots[q, 0], len(ms))

        def spread(flip):
            device, number = place.flipped(flip)
            remote(summed.at[number, piece], received.at[here, piece], plane_sem, recv_sem.at[q], device)

        for which in range(2):
            if first <= which * (plane // 2) < first + size:
                place.each_other(which, spread)
        if first + size == plane:
            pltpu.make_async_copy(summed.at[here, piece], received.at[here, piece], own_sem.at[q]).start()

    def written(q):
        rows_of = [pl.ds(s * (span * plane) + q * plane, plane) for s in range(2)]
        return [pltpu.make_async_copy(spectra.at[:, r], out.at[:, r], out_sem.at[q, s]) for s, r in enumerate(rows_of)]

    def assemble(q):
        ms = [m for (other, m) in slots if other == q]
        piece = pl.ds(slots[q, 0], len(ms))
        others = received.at[pl.ds(0, plane - 1), piece]
        pltpu.make_async_copy(others, others, recv_sem.at[q]).wait()
        pltpu.make_async_copy(summed.at[here, piece], received.at[here, piece], own_sem.at[q]).wait()

        @pl.loop(0, 4)
        def _(group):
            group_core, group_lo = group // 2, lax.rem(group, 2)
            column = group_lo * 2 + group_core
            for lane in range(half // 128):
                cols = pl.ds(lane * 128, 128)
                for part in range(2):
                    buffer = lane * 2 + part
                    for i in range(4 * RING):
                        line, m = part * 4 + i // RING, i % RING
                        value = received[group_core * 16 + line * 2 + group_lo, slots[q, m], :, cols].astype(jnp.float32)
                        if line and (q, m + RING) in slots:
                            value = value + received[group_core * 16 + (line - 1) * 2 + group_lo, slots[q, m + RING], :, cols].astype(jnp.float32)
                        turning[buffer, pl.ds(i * 8, 8), :] = value
                    for row in range(8):
                        picked = turning[buffer, pl.ds(row, 4 * RING, stride=8), :].astype(jnp.bfloat16)
                        rows_at = pl.ds((row % 2) * (span * plane) + q * plane + part * 4 * RING, 4 * RING)
                        spectra[row // 2, rows_at, pl.ds(pl.multiple_of(column * half + lane * 128, 128), 128)] = picked
        for copy in written(q):
            copy.start()

    at = []
    begin = 0
    arrived = 0
    for unit, outputs in enumerate(UNITS):
        count = len(outputs)
        while arrived <= min(span - 1, max(outputs)):
            for r in range(2):
                pltpu.make_async_copy(samples.at[arrived, r], samples.at[arrived, r], in_sem.at[arrived, r]).wait()
            arrived += 1
        inputs = [i for i in range(span) if any(0 <= f - i <= history for f in outputs)]

        @pl.loop(0, fine // rows)
        def _(step):
            here_rows = pl.ds(pl.multiple_of(step * rows, rows), rows)
            for r in range(2):
                for lane in range(half // 128):
                    cols = pl.ds(lane * 128, 128)
                    held = {i: samples[i, r, here_rows, cols].astype(jnp.float32) for i in inputs}
                    for place_in, f in enumerate(outputs):
                        total = None
                        for i in inputs:
                            if 0 <= f - i <= history:
                                term = wide_taps[f - i, here_rows] * held[i]
                                total = term if total is None else total + term
                        filtered[place_in, pl.ds(pl.multiple_of(r * fine + step * rows, rows), rows), cols] = total.astype(jnp.bfloat16)

        @pl.loop(0, count)
        def _(f):
            product = jnp.dot(table[...], filtered[f], preferred_element_type=jnp.float32)
            stage[begin + f] = product.astype(jnp.bfloat16).reshape(stage.shape[1:])

        at.append(pl.ds(begin, count))
        begin += count
        if unit < last:
            send(unit)
        else:
            send(last)
            send(last + 1)
        if unit >= 1:
            pass_on(unit - 1)
        if unit >= 2:
            finish(unit - 2)
        if unit >= FIRST_SUM + 4:
            assemble(UNITS[unit - 4][0] % span)

    for load in (last, last + 1):
        pass_on(load)
    finish(last - 1)
    for unit in (last - 3, last - 2):
        assemble(UNITS[unit][0] % span)
    for load in (last, last + 1):
        finish(load)
    for unit in (last - 1, last):
        assemble(UNITS[unit][0] % span)
    for copy in given:
        copy.wait_send()
    sent = stage.at[:, pl.ds(0, RING - 1)]
    pltpu.make_async_copy(sent, sent, send_sem).wait()
    pltpu.make_async_copy(relay, relay, pass_sem).wait()
    others = summed.at[pl.ds(0, plane - 1)]
    pltpu.make_async_copy(others, others, plane_sem).wait()
    for q in range(span):
        for copy in written(q):
            copy.wait()


def correlate(inverse, width, spectra, out, turned_in):
    depth, total_inputs = spectra.shape[1:]
    turned_in[pl.ds(0, depth // 2), :] = -spectra[0, pl.ds(depth // 2, depth // 2), :]
    turned_in[pl.ds(depth // 2, depth // 2), :] = spectra[0, pl.ds(0, depth // 2), :]
    upper = lax.broadcasted_iota(jnp.int32, (width, width), 0) <= lax.broadcasted_iota(jnp.int32, (width, width), 1)
    contract = (((0,), (0,)), ((), ()))
    for a in range(total_inputs // width):
        rows = pl.ds(a * width, width)
        left = spectra[0, :, rows]
        real = lax.dot_general(left, spectra[0, :, pl.ds(a * width, total_inputs - a * width)], contract, preferred_element_type=jnp.float32)
        imag = lax.dot_general(left, turned_in[:, pl.ds(0, (a + 1) * width)], contract, preferred_element_type=jnp.float32)
        if a:
            out[0, rows, pl.ds(0, a * width)] = (imag[:, : a * width] * inverse).astype(jnp.bfloat16)
        middle = jnp.where(upper, real[:, :width], imag[:, a * width :])
        out[0, rows, pl.ds(a * width, width)] = (middle * inverse).astype(jnp.bfloat16)
        if (a + 1) * width < total_inputs:
            out[0, rows, pl.ds((a + 1) * width, total_inputs - (a + 1) * width)] = (real[:, width:] * inverse).astype(jnp.bfloat16)


def per_device(voltages, taps):
    history = taps.shape[0] - 1
    fine = taps.shape[1]
    frames = voltages.shape[1] // fine
    width = voltages.shape[2]
    n_time = lax.axis_size("tm")
    n_group = lax.axis_size("inp")
    devices = n_time * n_group
    chans = KEEP // devices
    half = width // 2
    span = 2 * frames
    produced = span + history
    plane = devices // RING
    rows_kept = row_slots(span, history)[1]
    tables = [jnp.asarray(x) for x in table_parts(fine, KEEP, chans)]
    vmem = pl.BlockSpec(memory_space=pltpu.VMEM)
    hbm = pl.BlockSpec(memory_space=pl.ANY)
    block = (2 * chans, half)
    biggest = max(len(unit) for unit in UNITS)
    total = width * n_group
    depth = 2 * n_time * frames
    spectra = pl.pallas_call(
        functools.partial(spread_spectra, frames, fine, history),
        out_shape=jax.ShapeDtypeStruct((chans, depth, total), jnp.bfloat16),
        in_specs=[hbm] + [vmem] * 5,
        out_specs=hbm,
        scratch_shapes=[
            pltpu.VMEM((span, 2, fine, half), jnp.bfloat16),
            pltpu.VMEM((biggest, 2 * fine, half), jnp.bfloat16),
            pltpu.VMEM((produced, RING, plane, *block), jnp.bfloat16),
            pltpu.VMEM((produced, RING, plane, *block), jnp.bfloat16),
            pltpu.VMEM((produced, 2, plane // 2, *block), jnp.bfloat16),
            pltpu.VMEM((plane, rows_kept, *block), jnp.bfloat16),
            pltpu.VMEM((plane, rows_kept, *block), jnp.bfloat16),
            pltpu.VMEM((chans, depth, total), jnp.bfloat16),
            pltpu.VMEM((4, 128, 128), jnp.float32),
            pltpu.VMEM((2 * KEEP, 2 * fine), jnp.bfloat16),
            pltpu.VMEM((history + 1, fine, 128), jnp.float32),
            pltpu.SemaphoreType.DMA((span, 2)),
            pltpu.SemaphoreType.DMA((frames, 2)),
            pltpu.SemaphoreType.DMA,
            pltpu.SemaphoreType.DMA((len(UNITS) + 1,)),
            pltpu.SemaphoreType.DMA,
            pltpu.SemaphoreType.DMA((len(UNITS) + 1,)),
            pltpu.SemaphoreType.DMA((len(UNITS) + 1,)),
            pltpu.SemaphoreType.DMA,
            pltpu.SemaphoreType.DMA((span,)),
            pltpu.SemaphoreType.DMA((span,)),
            pltpu.SemaphoreType.DMA((span, 2)),
        ],
        compiler_params=pltpu.CompilerParams(collective_id=0, has_side_effects=True, vmem_limit_bytes=62 * 2**20),
        name="spread_spectra",
    )(voltages, taps.T, *tables)
    return pl.pallas_call(
        functools.partial(correlate, 1.0 / (n_time * frames), half),
        out_shape=jax.ShapeDtypeStruct((chans, total, total), jnp.bfloat16),
        grid=(chans,),
        in_specs=[pl.BlockSpec((1, depth, total), lambda c: (c, 0, 0))],
        out_specs=pl.BlockSpec((1, total, total), lambda c: (c, 0, 0)),
        scratch_shapes=[pltpu.VMEM((depth, total), jnp.bfloat16)],
        compiler_params=pltpu.CompilerParams(vmem_limit_bytes=32 * 2**20),
        name="correlate",
    )(spectra)


def solution(mesh):
    placed = (P(None, "tm", "inp"), P())
    return jax.shard_map(
        per_device,
        mesh=mesh,
        in_specs=placed,
        out_specs=P(("tm", "inp"), None, None),
        check_vma=False,
    )
```

```python
import functools
import math

import jax
import jax.numpy as jnp
import numpy as np
from jax import lax
from jax.experimental import pallas as pl
from jax.experimental.pallas import tpu as pltpu
from jax.sharding import PartitionSpec as P

KEEP = 512
MESH = pl.DeviceIdType.MESH


UNITS = ((0,), (1, 2), (8, 16), (9, 17), (10, 18), (3, 11), (4, 12), (5, 13), (6, 14), (7, 15))
FIRST_SUM = 2
RING = 4


def table_parts(fine, keep, owned):
    chan = (np.arange(keep) - keep // 2).reshape(-1, RING, 2, 2 * owned)
    chan = np.repeat(chan.transpose(1, 2, 0, 3).reshape(-1), 2)
    part = np.tile(np.arange(2), keep)
    low = (chan[:, None] * np.arange(128)[None, :] + part[:, None] * (fine // 4)) % fine
    turn = np.broadcast_to(((chan * 128) % fine)[:16, None], (16, 128))
    assert np.array_equal((chan * 128) % fine, np.tile(turn[:, 0], len(chan) // 16))
    scale = 1.0 / math.sqrt(fine)
    step = 2.0 * np.pi / fine
    return tuple(
        x.astype(np.float32) for x in (np.cos(step * low) * scale, np.sin(step * low) * scale, np.cos(step * turn), np.sin(step * turn))
    )


def row_slots(span, history):
    slots, count = {}, 0
    for q in range(span):
        for m in range(RING + (history + span - 1 - q) // span):
            slots[q, m] = count
            count += 1
    return slots, count


class Place:
    def __init__(self):
        time, self.z_lo = lax.axis_index("tm"), lax.axis_index("inp")
        self.core, self.y = lax.rem(time, 2), lax.rem(time // 2, RING)
        self.x, self.z_hi = lax.rem(time // 8, 4), time // 32

    def device(self, y, x, z_hi, core, z_lo):
        return {"tm": ((z_hi * 4 + x) * RING + y) * 2 + core, "inp": z_lo}

    def along(self, steps):
        return self.device(lax.rem(self.y + steps + RING, RING), self.x, self.z_hi, self.core, self.z_lo)

    def flipped(self, flip):
        x_flip, z_hi_flip, core_flip, z_lo_flip = flip
        x = lax.rem(self.x // 2 + x_flip // 2, 2) * 2 + lax.rem(self.x + x_flip, 2)
        z_hi = lax.rem(self.z_hi + z_hi_flip, 2)
        core, z_lo = lax.rem(self.core + core_flip, 2), lax.rem(self.z_lo + z_lo_flip, 2)
        return self.device(self.y, x, z_hi, core, z_lo), ((core * 2 + z_hi) * 4 + x) * 2 + z_lo

    def number(self):
        return ((self.core * 2 + self.z_hi) * 4 + self.x) * 2 + self.z_lo

    def each_other(self, core, action):
        core_flip = lax.rem(self.core + core, 2)

        @pl.loop(0, 8)
        def _(outer):
            for z_lo_flip in range(2):
                flip = (lax.rem(outer + 2, 4), 1 - outer // 4, core_flip, z_lo_flip)
                if z_lo_flip:
                    action(flip)
                else:
                    pl.when(flip[0] + flip[1] + core_flip > 0)(functools.partial(action, flip))


def spread_spectra(
    frames, fine, history, volt, taps, low_cos, low_sin, turn_cos, turn_sin, out,
    samples, filtered, stage, heard, relay, summed, received, spectra, turning, table, wide_taps,
    in_sem, give_sem, send_sem, relay_sem, pass_sem, heard_sem, keep_sem, plane_sem, recv_sem, own_sem, out_sem,
):
    place = Place()
    core, here = place.core, place.number()
    partner = lax.axis_index("tm") + 1 - 2 * core
    span = 2 * frames
    half = samples.shape[3]
    plane = summed.shape[0]
    slots, _ = row_slots(span, history)
    order = [f for unit in UNITS for f in unit]
    slot_of = {f: i for i, f in enumerate(order)}
    barrier = pltpu.get_barrier_semaphore()

    def greet(flip):
        pl.semaphore_signal(barrier, inc=1, device_id=place.flipped(flip)[0], device_id_type=MESH)

    for which in range(2):
        place.each_other(which, greet)
    for steps in (1, -1):
        pl.semaphore_signal(barrier, inc=1, device_id=place.along(steps), device_id_type=MESH)

    def lanes(which):
        return pl.ds(pl.multiple_of(which * half, half), half)

    pieces = [(f, r) for f in range(frames) for r in range(2)]
    for f, r in pieces:
        source = volt.at[r, pl.ds(f * fine, fine), lanes(core)]
        pltpu.make_async_copy(source, samples.at[core * frames + f, r], in_sem.at[core * frames + f, r]).start()

    rows = 16

    @pl.loop(0, table.shape[0] // rows)
    def _(step):
        at = pl.ds(pl.multiple_of(step * rows, rows), rows)
        now_cos, now_sin = low_cos[at, :], low_sin[at, :]
        by_cos, by_sin = turn_cos[...], turn_sin[...]
        for block in range(fine // 128):
            table[at, pl.ds(block * 128, 128)] = now_cos.astype(jnp.bfloat16)
            table[at, pl.ds(fine + block * 128, 128)] = now_sin.astype(jnp.bfloat16)
            now_cos, now_sin = now_cos * by_cos - now_sin * by_sin, now_sin * by_cos + now_cos * by_sin

    whole = taps[...].astype(jnp.float32).astype(jnp.bfloat16)
    tap_of = lax.broadcasted_iota(jnp.int32, (history + 1, 256), 0)
    lane_half = lax.broadcasted_iota(jnp.int32, (history + 1, 256), 1) // 128
    for k in range(0, history + 1, 2):
        pick = jnp.where(tap_of == k + lane_half, 1.0, 0.0).astype(jnp.bfloat16)
        wide = lax.dot_general(whole, pick, (((0,), (0,)), ((), ())), preferred_element_type=jnp.float32) * (1.0 / 8192.0)
        wide_taps[k] = wide[:, :128]
        wide_taps[k + 1] = wide[:, 128:]

    pl.semaphore_wait(barrier, plane + 1)

    given = []
    for f, r in pieces:
        given.append(
            pltpu.make_async_remote_copy(
                src_ref=volt.at[r, pl.ds(f * fine, fine), lanes(1 - core)],
                dst_ref=samples.at[core * frames + f, r],
                send_sem=give_sem.at[f, r],
                recv_sem=in_sem.at[core * frames + f, r],
                device_id={"tm": partner},
                device_id_type=MESH,
            )
        )
        given[-1].start()

    def remote(source, target, send, recv, device):
        pltpu.make_async_remote_copy(
            src_ref=source, dst_ref=target, send_sem=send, recv_sem=recv, device_id=device, device_id_type=MESH
        ).start()

    hops = ((0, 1), (1, -1))

    last = len(UNITS) - 1
    loads = [(unit, 0, plane) for unit in range(last)] + [(last, which * (plane // 2), plane // 2) for which in range(2)]

    def half_of(load, side):
        _, first, size = loads[load]
        return pl.ds(first + side * (size // 2), size // 2)

    def relayed(load):
        _, first, size = loads[load]
        return pl.ds(first // 2, size // 2)

    def send_far(load):
        unit = loads[load][0]
        across = lax.rem(place.y + 2, RING)
        for side, steps in hops:
            remote(stage.at[at[unit], across, half_of(load, side)], relay.at[at[unit], side, relayed(load)], send_sem, relay_sem.at[load], place.along(steps))

    def send_near(load):
        unit, first, size = loads[load]
        whole = pl.ds(first, size)
        for side, steps in hops:
            to = lax.rem(place.y + steps + RING, RING)
            remote(stage.at[at[unit], to, whole], heard.at[at[unit], place.y, whole], send_sem, heard_sem.at[load], place.along(steps))
        pltpu.make_async_copy(stage.at[at[unit], place.y, whole], heard.at[at[unit], place.y, whole], keep_sem.at[load]).start()

    def pass_on(load):
        unit = loads[load][0]
        came_in = relay.at[at[unit], :, relayed(load)]
        pltpu.make_async_copy(came_in, came_in, relay_sem.at[load]).wait()
        for side, steps in hops:
            came = lax.rem(place.y - steps + RING, RING)
            remote(
                relay.at[at[unit], side, relayed(load)], heard.at[at[unit], came, half_of(load, side)], pass_sem, heard_sem.at[load], place.along(steps)
            )

    done = set()

    def finish(load):
        unit, first, size = loads[load]
        whole = pl.ds(first, size)
        three = heard.at[at[unit], pl.ds(0, RING - 1), whole]
        pltpu.make_async_copy(three, three, heard_sem.at[load]).wait()
        one = heard.at[at[unit], 0, whole]
        pltpu.make_async_copy(one, one, keep_sem.at[load]).wait()
        if unit < FIRST_SUM:
            return
        q = UNITS[unit][0] % span
        ms = [m for (other, m) in slots if other == q]
        parts = list(range(q, span + history, span))

        @pl.loop(first, first + size)
        def _(device):
            for m in ms:
                total = None
                for j, f in enumerate(parts):
                    if 0 <= m - j < RING:
                        term = heard[slot_of[f], m - j, device].astype(jnp.float32)
                        total = term if total is None else total + term
                summed[device, slots[q, m]] = total.astype(jnp.bfloat16)

        piece = pl.ds(slots[q, 0], len(ms))

        def spread(flip):
            device, number = place.flipped(flip)
            remote(summed.at[number, piece], received.at[here, piece], plane_sem, recv_sem.at[q], device)

        for which in range(2):
            if first <= which * (plane // 2) < first + size:
                place.each_other(which, spread)
        if first + size == plane:
            pltpu.make_async_copy(summed.at[here, piece], received.at[here, piece], own_sem.at[q]).start()

    def written(q):
        rows_of = [pl.ds(s * (span * plane) + q * plane, plane) for s in range(2)]
        return [pltpu.make_async_copy(spectra.at[:, r], out.at[:, r], out_sem.at[q, s]) for s, r in enumerate(rows_of)]

    def assemble(q):
        ms = [m for (other, m) in slots if other == q]
        piece = pl.ds(slots[q, 0], len(ms))
        others = received.at[pl.ds(0, plane - 1), piece]
        pltpu.make_async_copy(others, others, recv_sem.at[q]).wait()
        pltpu.make_async_copy(summed.at[here, piece], received.at[here, piece], own_sem.at[q]).wait()

        @pl.loop(0, 4)
        def _(group):
            group_core, group_lo = group // 2, lax.rem(group, 2)
            column = group_lo * 2 + group_core
            for lane in range(half // 128):
                cols = pl.ds(lane * 128, 128)
                for part in range(2):
                    buffer = lane * 2 + part
                    for i in range(4 * RING):
                        line, m = part * 4 + i // RING, i % RING
                        value = received[group_core * 16 + line * 2 + group_lo, slots[q, m], :, cols].astype(jnp.float32)
                        if line and (q, m + RING) in slots:
                            value = value + received[group_core * 16 + (line - 1) * 2 + group_lo, slots[q, m + RING], :, cols].astype(jnp.float32)
                        turning[buffer, pl.ds(i * 8, 8), :] = value
                    for row in range(8):
                        picked = turning[buffer, pl.ds(row, 4 * RING, stride=8), :].astype(jnp.bfloat16)
                        rows_at = pl.ds((row % 2) * (span * plane) + q * plane + part * 4 * RING, 4 * RING)
                        spectra[row // 2, rows_at, pl.ds(pl.multiple_of(column * half + lane * 128, 128), 128)] = picked
        for copy in written(q):
            copy.start()

    at = []
    begin = 0
    arrived = 0
    for unit, outputs in enumerate(UNITS):
        count = len(outputs)
        while arrived <= min(span - 1, max(outputs)):
            for r in range(2):
                pltpu.make_async_copy(samples.at[arrived, r], samples.at[arrived, r], in_sem.at[arrived, r]).wait()
            arrived += 1
        inputs = [i for i in range(span) if any(0 <= f - i <= history for f in outputs)]

        @pl.loop(0, fine // rows)
        def _(step):
            here_rows = pl.ds(pl.multiple_of(step * rows, rows), rows)
            for r in range(2):
                for lane in range(half // 128):
                    cols = pl.ds(lane * 128, 128)
                    held = {i: samples[i, r, here_rows, cols].astype(jnp.float32) for i in inputs}
                    for place_in, f in enumerate(outputs):
                        total = None
                        for i in inputs:
                            if 0 <= f - i <= history:
                                term = wide_taps[f - i, here_rows] * held[i]
                                total = term if total is None else total + term
                        filtered[place_in, pl.ds(pl.multiple_of(r * fine + step * rows, rows), rows), cols] = total.astype(jnp.bfloat16)

        @pl.loop(0, count)
        def _(f):
            product = jnp.dot(table[...], filtered[f], preferred_element_type=jnp.float32)
            stage[begin + f] = product.astype(jnp.bfloat16).reshape(stage.shape[1:])

        at.append(pl.ds(begin, count))
        begin += count
        if unit >= 1:
            pass_on(unit - 1)
        send_far(unit)
        if unit == last:
            send_far(last + 1)
        send_near(unit)
        if unit >= 2:
            finish(unit - 2)
        if unit >= FIRST_SUM + 4:
            assemble(UNITS[unit - 4][0] % span)

    finish(last - 1)
    pass_on(last)
    send_near(last + 1)
    pass_on(last + 1)
    assemble(UNITS[last - 3][0] % span)
    finish(last)
    assemble(UNITS[last - 2][0] % span)
    finish(last + 1)
    for unit in (last - 1, last):
        assemble(UNITS[unit][0] % span)
    for copy in given:
        copy.wait_send()
    sent = stage.at[:, pl.ds(0, RING - 1)]
    pltpu.make_async_copy(sent, sent, send_sem).wait()
    pltpu.make_async_copy(relay, relay, pass_sem).wait()
    others = summed.at[pl.ds(0, plane - 1)]
    pltpu.make_async_copy(others, others, plane_sem).wait()
    for q in range(span):
        for copy in written(q):
            copy.wait()


def correlate(inverse, width, spectra, out, turned_in):
    depth, total_inputs = spectra.shape[1:]
    turned_in[pl.ds(0, depth // 2), :] = -spectra[0, pl.ds(depth // 2, depth // 2), :]
    turned_in[pl.ds(depth // 2, depth // 2), :] = spectra[0, pl.ds(0, depth // 2), :]
    upper = lax.broadcasted_iota(jnp.int32, (width, width), 0) <= lax.broadcasted_iota(jnp.int32, (width, width), 1)
    contract = (((0,), (0,)), ((), ()))
    for a in range(total_inputs // width):
        rows = pl.ds(a * width, width)
        left = spectra[0, :, rows]
        real = lax.dot_general(left, spectra[0, :, pl.ds(a * width, total_inputs - a * width)], contract, preferred_element_type=jnp.float32)
        imag = lax.dot_general(left, turned_in[:, pl.ds(0, (a + 1) * width)], contract, preferred_element_type=jnp.float32)
        if a:
            out[0, rows, pl.ds(0, a * width)] = (imag[:, : a * width] * inverse).astype(jnp.bfloat16)
        middle = jnp.where(upper, real[:, :width], imag[:, a * width :])
        out[0, rows, pl.ds(a * width, width)] = (middle * inverse).astype(jnp.bfloat16)
        if (a + 1) * width < total_inputs:
            out[0, rows, pl.ds((a + 1) * width, total_inputs - (a + 1) * width)] = (real[:, width:] * inverse).astype(jnp.bfloat16)


def per_device(voltages, taps):
    history = taps.shape[0] - 1
    fine = taps.shape[1]
    frames = voltages.shape[1] // fine
    width = voltages.shape[2]
    n_time = lax.axis_size("tm")
    n_group = lax.axis_size("inp")
    devices = n_time * n_group
    chans = KEEP // devices
    half = width // 2
    span = 2 * frames
    produced = span + history
    plane = devices // RING
    rows_kept = row_slots(span, history)[1]
    tables = [jnp.asarray(x) for x in table_parts(fine, KEEP, chans)]
    vmem = pl.BlockSpec(memory_space=pltpu.VMEM)
    hbm = pl.BlockSpec(memory_space=pl.ANY)
    block = (2 * chans, half)
    biggest = max(len(unit) for unit in UNITS)
    total = width * n_group
    depth = 2 * n_time * frames
    spectra = pl.pallas_call(
        functools.partial(spread_spectra, frames, fine, history),
        out_shape=jax.ShapeDtypeStruct((chans, depth, total), jnp.bfloat16),
        in_specs=[hbm] + [vmem] * 5,
        out_specs=hbm,
        scratch_shapes=[
            pltpu.VMEM((span, 2, fine, half), jnp.bfloat16),
            pltpu.VMEM((biggest, 2 * fine, half), jnp.bfloat16),
            pltpu.VMEM((produced, RING, plane, *block), jnp.bfloat16),
            pltpu.VMEM((produced, RING, plane, *block), jnp.bfloat16),
            pltpu.VMEM((produced, 2, plane // 2, *block), jnp.bfloat16),
            pltpu.VMEM((plane, rows_kept, *block), jnp.bfloat16),
            pltpu.VMEM((plane, rows_kept, *block), jnp.bfloat16),
            pltpu.VMEM((chans, depth, total), jnp.bfloat16),
            pltpu.VMEM((4, 128, 128), jnp.float32),
            pltpu.VMEM((2 * KEEP, 2 * fine), jnp.bfloat16),
            pltpu.VMEM((history + 1, fine, 128), jnp.float32),
            pltpu.SemaphoreType.DMA((span, 2)),
            pltpu.SemaphoreType.DMA((frames, 2)),
            pltpu.SemaphoreType.DMA,
            pltpu.SemaphoreType.DMA((len(UNITS) + 1,)),
            pltpu.SemaphoreType.DMA,
            pltpu.SemaphoreType.DMA((len(UNITS) + 1,)),
            pltpu.SemaphoreType.DMA((len(UNITS) + 1,)),
            pltpu.SemaphoreType.DMA,
            pltpu.SemaphoreType.DMA((span,)),
            pltpu.SemaphoreType.DMA((span,)),
            pltpu.SemaphoreType.DMA((span, 2)),
        ],
        compiler_params=pltpu.CompilerParams(collective_id=0, has_side_effects=True, vmem_limit_bytes=62 * 2**20),
        name="spread_spectra",
    )(voltages, taps, *tables)
    return pl.pallas_call(
        functools.partial(correlate, 1.0 / (n_time * frames), half),
        out_shape=jax.ShapeDtypeStruct((chans, total, total), jnp.bfloat16),
        grid=(chans,),
        in_specs=[pl.BlockSpec((1, depth, total), lambda c: (c, 0, 0))],
        out_specs=pl.BlockSpec((1, total, total), lambda c: (c, 0, 0)),
        scratch_shapes=[pltpu.VMEM((depth, total), jnp.bfloat16)],
        compiler_params=pltpu.CompilerParams(vmem_limit_bytes=62 * 2**20),
        name="correlate",
    )(spectra)


def solution(mesh):
    placed = (P(None, "tm", "inp"), P())
    return jax.shard_map(
        per_device,
        mesh=mesh,
        in_specs=placed,
        out_specs=P(("tm", "inp"), None, None),
        check_vma=False,
    )
```

```python
import functools
import math

import jax
import jax.numpy as jnp
import numpy as np
from jax import lax
from jax.experimental import pallas as pl
from jax.experimental.pallas import tpu as pltpu
from jax.sharding import PartitionSpec as P

KEEP = 512
MESH = pl.DeviceIdType.MESH


UNITS = ((0,), (1,), (8, 16), (9, 17), (2, 10, 18), (3, 11), (4, 12), (5, 13), (6, 14), (7, 15))
FIRST_SUM = 2
RING = 4


def table_parts(fine, keep, owned):
    chan = (np.arange(keep) - keep // 2).reshape(-1, RING, 2, 2 * owned)
    chan = np.repeat(chan.transpose(1, 2, 0, 3).reshape(-1), 2)
    part = np.tile(np.arange(2), keep)
    low = (chan[:, None] * np.arange(128)[None, :] + part[:, None] * (fine // 4)) % fine
    turn = np.broadcast_to(((chan * 128) % fine)[:16, None], (16, 128))
    assert np.array_equal((chan * 128) % fine, np.tile(turn[:, 0], len(chan) // 16))
    scale = 1.0 / math.sqrt(fine)
    step = 2.0 * np.pi / fine
    return tuple(
        x.astype(np.float32) for x in (np.cos(step * low) * scale, np.sin(step * low) * scale, np.cos(step * turn), np.sin(step * turn))
    )


def row_slots(span, history):
    slots, count = {}, 0
    for q in range(span):
        for m in range(RING + (history + span - 1 - q) // span):
            slots[q, m] = count
            count += 1
    return slots, count


class Place:
    def __init__(self):
        time, self.z_lo = lax.axis_index("tm"), lax.axis_index("inp")
        self.core, self.y = lax.rem(time, 2), lax.rem(time // 2, RING)
        self.x, self.z_hi = lax.rem(time // 8, 4), time // 32

    def device(self, y, x, z_hi, core, z_lo):
        return {"tm": ((z_hi * 4 + x) * RING + y) * 2 + core, "inp": z_lo}

    def along(self, steps):
        return self.device(lax.rem(self.y + steps + RING, RING), self.x, self.z_hi, self.core, self.z_lo)

    def flipped(self, flip):
        x_flip, z_hi_flip, core_flip, z_lo_flip = flip
        x = lax.rem(self.x // 2 + x_flip // 2, 2) * 2 + lax.rem(self.x + x_flip, 2)
        z_hi = lax.rem(self.z_hi + z_hi_flip, 2)
        core, z_lo = lax.rem(self.core + core_flip, 2), lax.rem(self.z_lo + z_lo_flip, 2)
        return self.device(self.y, x, z_hi, core, z_lo), ((core * 2 + z_hi) * 4 + x) * 2 + z_lo

    def number(self):
        return ((self.core * 2 + self.z_hi) * 4 + self.x) * 2 + self.z_lo

    def each_other(self, core, action):
        core_flip = lax.rem(self.core + core, 2)

        @pl.loop(0, 8)
        def _(outer):
            for z_lo_flip in range(2):
                flip = (lax.rem(outer + 2, 4), 1 - outer // 4, core_flip, z_lo_flip)
                if z_lo_flip:
                    action(flip)
                else:
                    pl.when(flip[0] + flip[1] + core_flip > 0)(functools.partial(action, flip))


def spread_spectra(
    frames, fine, history, volt, taps, low_cos, low_sin, turn_cos, turn_sin, out,
    samples, filtered, stage, heard, relay, summed, received, spectra, turning, table, wide_taps,
    in_sem, give_sem, send_sem, relay_sem, pass_sem, heard_sem, keep_sem, plane_sem, recv_sem, own_sem, out_sem,
):
    place = Place()
    core, here = place.core, place.number()
    partner = lax.axis_index("tm") + 1 - 2 * core
    span = 2 * frames
    half = samples.shape[3]
    plane = summed.shape[0]
    slots, _ = row_slots(span, history)
    order = [f for unit in UNITS for f in unit]
    slot_of = {f: i for i, f in enumerate(order)}
    barrier = pltpu.get_barrier_semaphore()

    def greet(flip):
        pl.semaphore_signal(barrier, inc=1, device_id=place.flipped(flip)[0], device_id_type=MESH)

    for which in range(2):
        place.each_other(which, greet)
    for steps in (1, -1):
        pl.semaphore_signal(barrier, inc=1, device_id=place.along(steps), device_id_type=MESH)

    def lanes(which):
        return pl.ds(pl.multiple_of(which * half, half), half)

    pieces = [(f, r) for f in range(frames) for r in range(2)]
    for f, r in pieces:
        source = volt.at[r, pl.ds(f * fine, fine), lanes(core)]
        pltpu.make_async_copy(source, samples.at[core * frames + f, r], in_sem.at[core * frames + f, r]).start()

    rows = 16

    @pl.loop(0, table.shape[0] // rows)
    def _(step):
        at = pl.ds(pl.multiple_of(step * rows, rows), rows)
        now_cos, now_sin = low_cos[at, :], low_sin[at, :]
        by_cos, by_sin = turn_cos[...], turn_sin[...]
        for block in range(fine // 128):
            table[at, pl.ds(block * 128, 128)] = now_cos.astype(jnp.bfloat16)
            table[at, pl.ds(fine + block * 128, 128)] = now_sin.astype(jnp.bfloat16)
            now_cos, now_sin = now_cos * by_cos - now_sin * by_sin, now_sin * by_cos + now_cos * by_sin

    whole = taps[...].astype(jnp.float32).astype(jnp.bfloat16)
    tap_of = lax.broadcasted_iota(jnp.int32, (history + 1, 256), 0)
    lane_half = lax.broadcasted_iota(jnp.int32, (history + 1, 256), 1) // 128
    for k in range(0, history + 1, 2):
        pick = jnp.where(tap_of == k + lane_half, 1.0, 0.0).astype(jnp.bfloat16)
        wide = lax.dot_general(whole, pick, (((0,), (0,)), ((), ())), preferred_element_type=jnp.float32) * (1.0 / 8192.0)
        wide_taps[k] = wide[:, :128]
        wide_taps[k + 1] = wide[:, 128:]

    pl.semaphore_wait(barrier, plane + 1)

    given = []
    for f, r in pieces:
        given.append(
            pltpu.make_async_remote_copy(
                src_ref=volt.at[r, pl.ds(f * fine, fine), lanes(1 - core)],
                dst_ref=samples.at[core * frames + f, r],
                send_sem=give_sem.at[f, r],
                recv_sem=in_sem.at[core * frames + f, r],
                device_id={"tm": partner},
                device_id_type=MESH,
            )
        )
        given[-1].start()

    def remote(source, target, send, recv, device):
        pltpu.make_async_remote_copy(
            src_ref=source, dst_ref=target, send_sem=send, recv_sem=recv, device_id=device, device_id_type=MESH
        ).start()

    hops = ((0, 1), (1, -1))

    last = len(UNITS) - 1
    loads = [(unit, 0, plane) for unit in range(last)] + [(last, which * (plane // 2), plane // 2) for which in range(2)]

    def half_of(load, side):
        _, first, size = loads[load]
        return pl.ds(first + side * (size // 2), size // 2)

    def relayed(load):
        _, first, size = loads[load]
        return pl.ds(first // 2, size // 2)

    def send_far(load):
        unit = loads[load][0]
        across = lax.rem(place.y + 2, RING)
        for side, steps in hops:
            remote(stage.at[at[unit], across, half_of(load, side)], relay.at[at[unit], side, relayed(load)], send_sem, relay_sem.at[load], place.along(steps))

    def send_near(load):
        unit, first, size = loads[load]
        whole = pl.ds(first, size)
        for side, steps in hops:
            to = lax.rem(place.y + steps + RING, RING)
            remote(stage.at[at[unit], to, whole], heard.at[at[unit], place.y, whole], send_sem, heard_sem.at[load], place.along(steps))
        pltpu.make_async_copy(stage.at[at[unit], place.y, whole], heard.at[at[unit], place.y, whole], keep_sem.at[load]).start()

    def pass_on(load):
        unit = loads[load][0]
        came_in = relay.at[at[unit], :, relayed(load)]
        pltpu.make_async_copy(came_in, came_in, relay_sem.at[load]).wait()
        for side, steps in hops:
            came = lax.rem(place.y - steps + RING, RING)
            remote(
                relay.at[at[unit], side, relayed(load)], heard.at[at[unit], came, half_of(load, side)], pass_sem, heard_sem.at[load], place.along(steps)
            )

    done = set()

    def finish(load):
        unit, first, size = loads[load]
        whole = pl.ds(first, size)
        three = heard.at[at[unit], pl.ds(0, RING - 1), whole]
        pltpu.make_async_copy(three, three, heard_sem.at[load]).wait()
        one = heard.at[at[unit], 0, whole]
        pltpu.make_async_copy(one, one, keep_sem.at[load]).wait()
        if unit < FIRST_SUM:
            return
        q = UNITS[unit][0] % span
        ms = [m for (other, m) in slots if other == q]
        parts = list(range(q, span + history, span))

        @pl.loop(first, first + size)
        def _(device):
            for m in ms:
                total = None
                for j, f in enumerate(parts):
                    if 0 <= m - j < RING:
                        term = heard[slot_of[f], m - j, device].astype(jnp.float32)
                        total = term if total is None else total + term
                summed[device, slots[q, m]] = total.astype(jnp.bfloat16)

        piece = pl.ds(slots[q, 0], len(ms))

        def spread(flip):
            device, number = place.flipped(flip)
            remote(summed.at[number, piece], received.at[here, piece], plane_sem, recv_sem.at[q], device)

        for which in range(2):
            if first <= which * (plane // 2) < first + size:
                place.each_other(which, spread)
        if first + size == plane:
            pltpu.make_async_copy(summed.at[here, piece], received.at[here, piece], own_sem.at[q]).start()

    def written(q):
        rows_of = [pl.ds(s * (span * plane) + q * plane, plane) for s in range(2)]
        return [pltpu.make_async_copy(spectra.at[:, r], out.at[:, r], out_sem.at[q, s]) for s, r in enumerate(rows_of)]

    def assemble(q):
        ms = [m for (other, m) in slots if other == q]
        piece = pl.ds(slots[q, 0], len(ms))
        others = received.at[pl.ds(0, plane - 1), piece]
        pltpu.make_async_copy(others, others, recv_sem.at[q]).wait()
        pltpu.make_async_copy(summed.at[here, piece], received.at[here, piece], own_sem.at[q]).wait()

        @pl.loop(0, 4)
        def _(group):
            group_core, group_lo = group // 2, lax.rem(group, 2)
            column = group_lo * 2 + group_core
            for lane in range(half // 128):
                cols = pl.ds(lane * 128, 128)
                for part in range(2):
                    buffer = lane * 2 + part
                    for i in range(4 * RING):
                        line, m = part * 4 + i // RING, i % RING
                        value = received[group_core * 16 + line * 2 + group_lo, slots[q, m], :, cols].astype(jnp.float32)
                        if line and (q, m + RING) in slots:
                            value = value + received[group_core * 16 + (line - 1) * 2 + group_lo, slots[q, m + RING], :, cols].astype(jnp.float32)
                        turning[buffer, pl.ds(i * 8, 8), :] = value
                    for row in range(8):
                        picked = turning[buffer, pl.ds(row, 4 * RING, stride=8), :].astype(jnp.bfloat16)
                        rows_at = pl.ds((row % 2) * (span * plane) + q * plane + part * 4 * RING, 4 * RING)
                        spectra[row // 2, rows_at, pl.ds(pl.multiple_of(column * half + lane * 128, 128), 128)] = picked
        for copy in written(q):
            copy.start()

    at = []
    begin = 0
    arrived = 0
    for unit, outputs in enumerate(UNITS):
        count = len(outputs)
        while arrived <= min(span - 1, max(outputs)):
            for r in range(2):
                pltpu.make_async_copy(samples.at[arrived, r], samples.at[arrived, r], in_sem.at[arrived, r]).wait()
            arrived += 1
        inputs = [i for i in range(span) if any(0 <= f - i <= history for f in outputs)]

        @pl.loop(0, fine // rows)
        def _(step):
            here_rows = pl.ds(pl.multiple_of(step * rows, rows), rows)
            for r in range(2):
                for lane in range(half // 128):
                    cols = pl.ds(lane * 128, 128)
                    held = {i: samples[i, r, here_rows, cols].astype(jnp.float32) for i in inputs}
                    for place_in, f in enumerate(outputs):
                        total = None
                        for i in inputs:
                            if 0 <= f - i <= history:
                                term = wide_taps[f - i, here_rows] * held[i]
                                total = term if total is None else total + term
                        filtered[place_in, pl.ds(pl.multiple_of(r * fine + step * rows, rows), rows), cols] = total.astype(jnp.bfloat16)

        @pl.loop(0, count)
        def _(f):
            product = jnp.dot(table[...], filtered[f], preferred_element_type=jnp.float32)
            stage[begin + f] = product.astype(jnp.bfloat16).reshape(stage.shape[1:])

        at.append(pl.ds(begin, count))
        begin += count
        if unit >= 1:
            pass_on(unit - 1)
        send_far(unit)
        if unit == last:
            send_far(last + 1)
        send_near(unit)
        if unit >= 2:
            finish(unit - 2)
        if unit >= FIRST_SUM + 4:
            assemble(UNITS[unit - 4][0] % span)

    finish(last - 1)
    pass_on(last)
    send_near(last + 1)
    pass_on(last + 1)
    assemble(UNITS[last - 3][0] % span)
    finish(last)
    assemble(UNITS[last - 2][0] % span)
    finish(last + 1)
    for unit in (last - 1, last):
        assemble(UNITS[unit][0] % span)
    for copy in given:
        copy.wait_send()
    sent = stage.at[:, pl.ds(0, RING - 1)]
    pltpu.make_async_copy(sent, sent, send_sem).wait()
    pltpu.make_async_copy(relay, relay, pass_sem).wait()
    others = summed.at[pl.ds(0, plane - 1)]
    pltpu.make_async_copy(others, others, plane_sem).wait()
    for q in range(span):
        for copy in written(q):
            copy.wait()


def correlate(inverse, width, spectra, out, turned_in):
    depth, total_inputs = spectra.shape[1:]
    turned_in[pl.ds(0, depth // 2), :] = -spectra[0, pl.ds(depth // 2, depth // 2), :]
    turned_in[pl.ds(depth // 2, depth // 2), :] = spectra[0, pl.ds(0, depth // 2), :]
    upper = lax.broadcasted_iota(jnp.int32, (width, width), 0) <= lax.broadcasted_iota(jnp.int32, (width, width), 1)
    contract = (((0,), (0,)), ((), ()))
    for a in range(total_inputs // width):
        rows = pl.ds(a * width, width)
        left = spectra[0, :, rows]
        real = lax.dot_general(left, spectra[0, :, pl.ds(a * width, total_inputs - a * width)], contract, preferred_element_type=jnp.float32)
        imag = lax.dot_general(left, turned_in[:, pl.ds(0, (a + 1) * width)], contract, preferred_element_type=jnp.float32)
        if a:
            out[0, rows, pl.ds(0, a * width)] = (imag[:, : a * width] * inverse).astype(jnp.bfloat16)
        middle = jnp.where(upper, real[:, :width], imag[:, a * width :])
        out[0, rows, pl.ds(a * width, width)] = (middle * inverse).astype(jnp.bfloat16)
        if (a + 1) * width < total_inputs:
            out[0, rows, pl.ds((a + 1) * width, total_inputs - (a + 1) * width)] = (real[:, width:] * inverse).astype(jnp.bfloat16)


def per_device(voltages, taps):
    history = taps.shape[0] - 1
    fine = taps.shape[1]
    frames = voltages.shape[1] // fine
    width = voltages.shape[2]
    n_time = lax.axis_size("tm")
    n_group = lax.axis_size("inp")
    devices = n_time * n_group
    chans = KEEP // devices
    half = width // 2
    span = 2 * frames
    produced = span + history
    plane = devices // RING
    rows_kept = row_slots(span, history)[1]
    tables = [jnp.asarray(x) for x in table_parts(fine, KEEP, chans)]
    vmem = pl.BlockSpec(memory_space=pltpu.VMEM)
    hbm = pl.BlockSpec(memory_space=pl.ANY)
    block = (2 * chans, half)
    biggest = max(len(unit) for unit in UNITS)
    total = width * n_group
    depth = 2 * n_time * frames
    spectra = pl.pallas_call(
        functools.partial(spread_spectra, frames, fine, history),
        out_shape=jax.ShapeDtypeStruct((chans, depth, total), jnp.bfloat16),
        in_specs=[hbm] + [vmem] * 5,
        out_specs=hbm,
        scratch_shapes=[
            pltpu.VMEM((span, 2, fine, half), jnp.bfloat16),
            pltpu.VMEM((biggest, 2 * fine, half), jnp.bfloat16),
            pltpu.VMEM((produced, RING, plane, *block), jnp.bfloat16),
            pltpu.VMEM((produced, RING, plane, *block), jnp.bfloat16),
            pltpu.VMEM((produced, 2, plane // 2, *block), jnp.bfloat16),
            pltpu.VMEM((plane, rows_kept, *block), jnp.bfloat16),
            pltpu.VMEM((plane, rows_kept, *block), jnp.bfloat16),
            pltpu.VMEM((chans, depth, total), jnp.bfloat16),
            pltpu.VMEM((4, 128, 128), jnp.float32),
            pltpu.VMEM((2 * KEEP, 2 * fine), jnp.bfloat16),
            pltpu.VMEM((history + 1, fine, 128), jnp.float32),
            pltpu.SemaphoreType.DMA((span, 2)),
            pltpu.SemaphoreType.DMA((frames, 2)),
            pltpu.SemaphoreType.DMA,
            pltpu.SemaphoreType.DMA((len(UNITS) + 1,)),
            pltpu.SemaphoreType.DMA,
            pltpu.SemaphoreType.DMA((len(UNITS) + 1,)),
            pltpu.SemaphoreType.DMA((len(UNITS) + 1,)),
            pltpu.SemaphoreType.DMA,
            pltpu.SemaphoreType.DMA((span,)),
            pltpu.SemaphoreType.DMA((span,)),
            pltpu.SemaphoreType.DMA((span, 2)),
        ],
        compiler_params=pltpu.CompilerParams(collective_id=0, has_side_effects=True, vmem_limit_bytes=62 * 2**20),
        name="spread_spectra",
    )(voltages, taps, *tables)
    return pl.pallas_call(
        functools.partial(correlate, 1.0 / (n_time * frames), half),
        out_shape=jax.ShapeDtypeStruct((chans, total, total), jnp.bfloat16),
        grid=(chans,),
        in_specs=[pl.BlockSpec((1, depth, total), lambda c: (c, 0, 0))],
        out_specs=pl.BlockSpec((1, total, total), lambda c: (c, 0, 0)),
        scratch_shapes=[pltpu.VMEM((depth, total), jnp.bfloat16)],
        compiler_params=pltpu.CompilerParams(vmem_limit_bytes=62 * 2**20),
        name="correlate",
    )(spectra)


def solution(mesh):
    placed = (P(None, "tm", "inp"), P())
    return jax.shard_map(
        per_device,
        mesh=mesh,
        in_specs=placed,
        out_specs=P(("tm", "inp"), None, None),
        check_vma=False,
    )
```
